32 devices in a mesh: lon: 8 (over y, x, core), lat: 4 (over z).
Axes of the slice: x: 2, y: 2, z: 4, core: 2. Of those that a mesh axis runs over, the one named last changes fastest.
Arguments:
- gradient: float32 [137, 16, 1024], P(None, 'lat', 'lon'), may hold values from -60 to 60
- obs_weight: float32 [137, 16, 1024], P(None, 'lat', 'lon'), may hold values from 0.2 to 5
- half_width: int32 [16], P('lat'), may hold values from 8 to 32
- zonal_coef: float32 [16, 33], P('lat'), may hold values from 0.2 to 1
- mirror_map: int32 [1024], P('lon'), may hold values from 0 to 1023, as said below
- merid_coef: float32 [5], replicated, may hold values from 0.2 to 1
- vertical_map: float32 [137, 137], replicated, may hold values from -0.5 to 0.5
Outputs:
- increment: float32 [137, 16, 1024], P(None, 'lat', 'lon')
- residual: float32 [137, 16, 1024], P(None, 'lat', 'lon')
The draws below stay inside these ranges and needn't reach their ends.
Inputs may be any that keep to these rules, and one draw needn't show every extreme that they name: mirror_map[mirror_map[i]] = i, and mirror_map[i] lies in the block of 128 longitudes whose block index differs from i // 128 by 4.
All inputs are finite; a program needn't handle non-finite values.
Results may differ from the reference program's by a relative error of at most 0.04.
Values sent between devices are 32-bit elements; how exact they have to be, the bound alone decides.
No kernel may reach another device: no remote copies, remote signals or barrier semaphores. Data moves between devices by JAX's collectives and lax.ppermute only.
A program may use at most 64 MiB of HBM per device.

```python
import math
import jax
import jax.numpy as jnp
from jax import lax

LEV = 137
LON_DEV = 128
HMAX = 32
MDEPTH = 4
OUTER = 2
NLAT = 16
NLON = 1024


def draw_gradient(key, part):
    lat_ids = jnp.arange(NLAT, dtype=jnp.float32)
    lon_ids = jnp.arange(NLON, dtype=jnp.float32)
    lat_factor = jnp.exp(math.log(3.0) * (lat_ids / NLAT))
    lon_factor = jnp.exp(math.log(3.0) * (lon_ids / NLON))
    amplitude = lat_factor[:, None] * lon_factor[None, :]
    noise = jnp.clip(jax.random.normal(key, (LEV, NLAT, NLON), jnp.float32), -3.0, 3.0)
    return (noise * amplitude[None]).astype(jnp.float32)


def draw_half_width(key, part):
    row_ids = jnp.arange(NLAT, dtype=jnp.int32)
    pole_dist = jnp.minimum(row_ids, NLAT - 1 - row_ids)
    base_width = HMAX // (1 + 8 * pole_dist // NLAT)
    jitter = jax.random.randint(key, (NLAT,), 0, 3, dtype=jnp.int32)
    jitter = jnp.where(pole_dist == NLAT // 2 - 1, 0, jitter)
    return jnp.minimum(HMAX, base_width + jitter).astype(jnp.int32)


def draw_mirror_map(key, part):
    block_count = NLON // LON_DEV
    halfway = block_count // 2
    key_list = jax.random.split(key, halfway)
    permuted = jax.vmap(lambda one_key: jax.random.permutation(one_key, LON_DEV))(key_list).astype(jnp.int32)
    inverse = jnp.argsort(permuted, axis=1, stable=True).astype(jnp.int32)
    block_ids = jnp.arange(halfway, dtype=jnp.int32)
    low_part = permuted + ((block_ids + halfway) * LON_DEV)[:, None]
    high_part = inverse + (block_ids * LON_DEV)[:, None]
    return jnp.concatenate([low_part, high_part], axis=0).reshape(NLON).astype(jnp.int32)


def steps_of(rng, dims, shards, least, largest):
    def one(position, blocks):
        steps = jax.random.uniform(jax.random.fold_in(jax.random.fold_in(rng, 6), position), (blocks,), jnp.float32, least / len(shards), largest / len(shards))
        return jnp.repeat(jnp.exp(steps), dims[position] // blocks).reshape((-1,) + (1,) * (len(dims) - position - 1))

    level = one(*shards[0])
    for cut in shards[1:]:
        level = level * one(*cut)
    return level


def normal_values(own_key, extent, deviation, most, held_as=jnp.bfloat16):
    entries = deviation * jax.random.normal(own_key, extent, jnp.float32)
    return jnp.clip(entries, min=-most, max=most).astype(held_as)


def setup_inputs(seed: int = 0) -> dict:
    key_of = jax.random.split(jax.random.key(seed), 8)
    return {
        "gradient": draw_gradient(jax.random.fold_in(key_of[7], 71), 0),
        "obs_weight": jnp.clip(jnp.exp(math.log(5.0) - 3.218876 * jax.random.uniform(key_of[1], (LEV, NLAT, NLON), jnp.float32) ** steps_of(key_of[1], (LEV, NLAT, NLON), ((1, 4), (2, 8)), -0.2, 0.2)), 0.2, 5.0),
        "half_width": draw_half_width(jax.random.fold_in(key_of[7], 71), 0),
        "zonal_coef": jnp.clip(0.2 + 0.8 * jax.random.uniform(key_of[3], (NLAT, HMAX + 1), jnp.float32) ** steps_of(key_of[3], (NLAT, HMAX + 1), ((0, 4),), -0.2, 0.2), 0.2, 1.0),
        "mirror_map": draw_mirror_map(jax.random.fold_in(key_of[7], 71), 0),
        "merid_coef": jnp.clip(jax.random.uniform(key_of[5], (MDEPTH + 1,), jnp.float32, 0.2, 1.0), 0.2, 1.0),
        "vertical_map": normal_values(key_of[6], (LEV, LEV), LEV ** -0.5, 0.5, jnp.float32),
    }


def zonal_weights(half_width, zonal_coef):
    tap_ids = jnp.arange(zonal_coef.shape[1], dtype=jnp.int32)
    kept = jnp.where(tap_ids[None, :] <= half_width[:, None], zonal_coef, jnp.zeros_like(zonal_coef))
    scaling = jnp.sqrt(kept[:, 0] ** 2 + 2.0 * lax.optimization_barrier(jnp.sum(kept[:, 1:] ** 2, axis=1)))
    return kept / scaling[:, None]

def merid_weights(merid_coef):
    norm_value = jnp.sqrt(merid_coef[0] ** 2 + 2.0 * jnp.sum(merid_coef[1:] ** 2))
    return merid_coef / norm_value

def zonal_full(field_in, weights):
    width = weights.shape[1] - 1
    start = weights[:, 0][None, :, None] * field_in

    def add_tap(offset, summed):
        coef_col = lax.dynamic_slice_in_dim(weights, offset, 1, 1)[None]
        return summed + coef_col * (jnp.roll(field_in, offset, axis=2) + jnp.roll(field_in, -offset, axis=2))
    return lax.fori_loop(1, width + 1, add_tap, start)

def merid_full(field_in, weights, mirror_map):
    rim_depth = weights.shape[0] - 1
    row_count = field_in.shape[1]
    north_rows = jnp.flip(field_in[:, :rim_depth], axis=1)[:, :, mirror_map]
    south_rows = jnp.flip(field_in[:, row_count - rim_depth:], axis=1)[:, :, mirror_map]
    extended = jnp.concatenate([north_rows, field_in, south_rows], axis=1)
    result = weights[0] * field_in
    for offset in range(1, rim_depth + 1):
        upper = extended[:, rim_depth - offset:rim_depth - offset + row_count]
        lower = extended[:, rim_depth + offset:rim_depth + offset + row_count]
        result = result + weights[offset] * (upper + lower)
    return result

def hessian(vector, obs_weight, zonal_w, merid_w, mirror_map, vertical_map):
    forward = merid_full(zonal_full(vector, zonal_w), merid_w, mirror_map)
    lifted = jnp.einsum('kl,lji->kji', vertical_map, forward, precision=lax.Precision.HIGHEST)
    lowered = jnp.einsum('lk,lji->kji', vertical_map, obs_weight * lifted, precision=lax.Precision.HIGHEST)
    back = zonal_full(merid_full(lowered, merid_w, mirror_map), zonal_w)
    return vector + back

def reference(gradient, obs_weight, half_width, zonal_coef, mirror_map, merid_coef, vertical_map):
    zonal_w = zonal_weights(half_width, zonal_coef)
    merid_w = merid_weights(merid_coef)
    increment = jnp.zeros_like(gradient)
    residual = gradient
    for outer in range(OUTER):
        first = hessian(residual, obs_weight, zonal_w, merid_w, mirror_map, vertical_map)
        second = hessian(first, obs_weight, zonal_w, merid_w, mirror_map, vertical_map)
        sum_rr = jnp.sum(residual * residual)
        sum_rf = jnp.sum(residual * first)
        sum_ff = jnp.sum(first * first)
        sum_fs = jnp.sum(first * second)
        determinant = sum_rf * sum_fs - sum_ff * sum_ff
        coef_one = (sum_fs * sum_rr - sum_ff * sum_rf) / determinant
        coef_two = (sum_rf * sum_rf - sum_ff * sum_rr) / determinant
        increment = increment + coef_one * residual + coef_two * first
        residual = residual - coef_one * first - coef_two * second
    return (increment, residual)
```

```python
import jax
import jax.numpy as jnp
from jax import lax
from jax.sharding import PartitionSpec as P

OUTER = 2
AXES = ("lon", "lat")
HI = lax.Precision.HIGHEST


def zonal_weights(half_width, zonal_coef):
    tap_ids = jnp.arange(zonal_coef.shape[1], dtype=jnp.int32)
    kept = jnp.where(
        tap_ids[None, :] <= half_width[:, None], zonal_coef, jnp.zeros_like(zonal_coef)
    )
    scaling = jnp.sqrt(kept[:, 0] ** 2 + 2.0 * jnp.sum(kept[:, 1:] ** 2, axis=1))
    return kept / scaling[:, None]


def merid_weights(merid_coef):
    norm_value = jnp.sqrt(merid_coef[0] ** 2 + 2.0 * jnp.sum(merid_coef[1:] ** 2))
    return merid_coef / norm_value


def zonal_tables(weights, block):
    width = weights.shape[1] - 1
    positions = jnp.arange(block + 2 * width, dtype=jnp.int32)
    columns = jnp.arange(block, dtype=jnp.int32)
    tap_ids = jnp.arange(width + 1, dtype=jnp.int32)
    distance = jnp.abs(positions[:, None] - width - columns[None, :])
    selector = (distance[:, :, None] == tap_ids[None, None, :]).astype(jnp.float32)
    return jnp.einsum("pct,jt->jpc", selector, weights, precision=HI)


def zonal_level(field_in, table, block):
    lev, rows, nlon = field_in.shape
    width = (table.shape[1] - block) // 2
    blocks = field_in.reshape(lev, rows, nlon // block, block)
    before = jnp.roll(blocks, 1, axis=2)[..., block - width :]
    after = jnp.roll(blocks, -1, axis=2)[..., :width]
    padded = jnp.concatenate([before, blocks, after], axis=3)
    out = jnp.einsum("ljbp,jpc->ljbc", padded, table, precision=HI)
    return out.reshape(lev, rows, nlon)


def merid_level(field_in, weights, mirror_map):
    rim_depth = weights.shape[0] - 1
    row_count = field_in.shape[1]
    north_rows = jnp.take(jnp.flip(field_in[:, :rim_depth], axis=1), mirror_map, axis=2)
    south_rows = jnp.take(
        jnp.flip(field_in[:, row_count - rim_depth :], axis=1), mirror_map, axis=2
    )
    extended = jnp.concatenate([north_rows, field_in, south_rows], axis=1)
    result = weights[0] * field_in
    for offset in range(1, rim_depth + 1):
        upper = extended[:, rim_depth - offset : rim_depth - offset + row_count]
        lower = extended[:, rim_depth + offset : rim_depth + offset + row_count]
        result = result + weights[offset] * (upper + lower)
    return result


def per_device(gradient, obs_weight, half_width, zonal_coef, mirror_map, merid_coef, vertical_map):
    n_lon = lax.axis_size("lon")
    n_lat = lax.axis_size("lat")
    n_dev = n_lon * n_lat
    lev, rows, cols = gradient.shape
    per = -(-lev // n_dev)
    width = zonal_coef.shape[1] - 1
    merid_w = merid_weights(merid_coef)

    def exchange(parts):
        return lax.all_to_all(parts, AXES, 0, 0, tiled=True)

    def col_parts(x):
        x = jnp.pad(x, ((0, n_dev * per - lev), (0, 0), (0, 0)))
        return x.reshape(n_dev, per, rows, cols)

    def to_level(z):
        z = z.reshape(n_lon, n_lat, per, rows, cols).transpose(2, 1, 3, 0, 4)
        return z.reshape(per, n_lat * rows, n_lon * cols)

    def level_parts(v):
        v = v.reshape(per, n_lat, rows, n_lon, cols).transpose(3, 1, 0, 2, 4)
        return v.reshape(n_dev, per, rows, cols)

    def to_column(z):
        return z.reshape(n_dev * per, rows, cols)[:lev]

    def slab(values):
        flat = jnp.zeros((rows * cols,), jnp.float32).at[: values.shape[0]].set(values)
        return jnp.broadcast_to(flat.reshape(1, 1, rows, cols), (n_dev, 1, rows, cols))

    mirror_slab = jnp.zeros((1, 1, rows, cols), jnp.float32).at[0, 0, 0].set(
        mirror_map.astype(jnp.float32)
    )
    zonal_slab = jnp.zeros((1, 1, rows, cols), jnp.float32).at[0, 0, :, : width + 1].set(
        zonal_weights(half_width, zonal_coef)
    )
    got = exchange(
        jnp.concatenate(
            [
                col_parts(gradient),
                jnp.broadcast_to(mirror_slab, (n_dev, 1, rows, cols)),
                jnp.broadcast_to(zonal_slab, (n_dev, 1, rows, cols)),
            ],
            axis=1,
        )
    )
    residual = to_level(got[:, :per])
    mirror_all = (
        got[:, per, 0, :].reshape(n_lon, n_lat, cols)[:, 0].reshape(n_lon * cols).astype(jnp.int32)
    )
    zonal_all = (
        got[:, per + 1, :, : width + 1]
        .reshape(n_lon, n_lat, rows, width + 1)[0]
        .reshape(n_lat * rows, width + 1)
    )
    table = zonal_tables(zonal_all, cols)

    def forward(x):
        return merid_level(zonal_level(x, table, cols), merid_w, mirror_all)

    def backward(g):
        return zonal_level(merid_level(g, merid_w, mirror_all), table, cols)

    def middle(y):
        lifted = jnp.einsum("kl,lji->kji", vertical_map, y, precision=HI)
        return jnp.einsum("lk,lji->kji", vertical_map, obs_weight * lifted, precision=HI)

    def image(x, px_col):
        return x + backward(to_level(exchange(col_parts(middle(px_col)))))

    res_col = gradient
    inc_col = jnp.zeros_like(gradient)
    pres_col = to_column(exchange(level_parts(forward(residual))))
    for outer in range(OUTER):
        last = outer == OUTER - 1
        first = image(residual, pres_col)
        got = exchange(jnp.concatenate([level_parts(forward(first)), level_parts(first)], axis=1))
        pfirst_col = to_column(got[:, :per])
        first_col = to_column(got[:, per:])
        second = image(first, pfirst_col)
        sums = jnp.stack(
            [
                jnp.sum(residual * residual),
                jnp.sum(residual * first),
                jnp.sum(first * first),
                jnp.sum(first * second),
            ]
        )
        parts = [level_parts(second)]
        if not last:
            parts.append(level_parts(forward(second)))
        got = exchange(jnp.concatenate(parts + [slab(sums)], axis=1))
        second_col = to_column(got[:, :per])
        total = jnp.sum(got[:, len(parts) * per, 0, : sums.shape[0]], axis=0)
        sum_rr, sum_rf, sum_ff, sum_fs = total[0], total[1], total[2], total[3]
        determinant = sum_rf * sum_fs - sum_ff * sum_ff
        coef_one = (sum_fs * sum_rr - sum_ff * sum_rf) / determinant
        coef_two = (sum_rf * sum_rf - sum_ff * sum_rr) / determinant
        inc_col = inc_col + coef_one * res_col + coef_two * first_col
        res_col = res_col - coef_one * first_col - coef_two * second_col
        if not last:
            psecond_col = to_column(got[:, per : 2 * per])
            residual = residual - coef_one * first - coef_two * second
            pres_col = pres_col - coef_one * pfirst_col - coef_two * psecond_col
    return (inc_col, res_col)


def solution(mesh):
    placed = (
        P(None, "lat", "lon"),
        P(None, "lat", "lon"),
        P("lat"),
        P("lat", None),
        P("lon"),
        P(),
        P(),
    )
    return jax.shard_map(
        per_device,
        mesh=mesh,
        in_specs=placed,
        out_specs=(P(None, "lat", "lon"), P(None, "lat", "lon")),
        check_vma=False,
    )
```

```python
import functools

import jax
import jax.numpy as jnp
from jax import lax
from jax.experimental import pallas as pl
from jax.experimental.pallas import tpu as pltpu
from jax.sharding import PartitionSpec as P

OUTER = 2
AXES = ("lon", "lat")
HI = lax.Precision.HIGHEST


def zonal_weights(half_width, zonal_coef):
    tap_ids = jnp.arange(zonal_coef.shape[1], dtype=jnp.int32)
    kept = jnp.where(
        tap_ids[None, :] <= half_width[:, None], zonal_coef, jnp.zeros_like(zonal_coef)
    )
    scaling = jnp.sqrt(kept[:, 0] ** 2 + 2.0 * jnp.sum(kept[:, 1:] ** 2, axis=1))
    return kept / scaling[:, None]


def merid_weights(merid_coef):
    norm_value = jnp.sqrt(merid_coef[0] ** 2 + 2.0 * jnp.sum(merid_coef[1:] ** 2))
    return merid_coef / norm_value


def zonal_tables(weights, block):
    width = weights.shape[1] - 1
    positions = jnp.arange(3 * block, dtype=jnp.int32)
    columns = jnp.arange(block, dtype=jnp.int32)
    tap_ids = jnp.arange(width + 1, dtype=jnp.int32)
    distance = jnp.abs(positions[:, None] - block - columns[None, :])
    selector = (distance[:, :, None] == tap_ids[None, None, :]).astype(jnp.float32)
    table = jnp.einsum("pct,jt->jpc", selector, weights, precision=HI)
    return table.reshape(weights.shape[0], 3, block, block)


def mirror_tables(mirror_all, block):
    return (mirror_all % block).reshape(mirror_all.shape[0] // block, block)


def _zonal_rows(src, dst, table_ref, nb):
    rows, _, lp, block = src.shape
    for j in range(rows):
        mid = src[j]
        prev = jnp.concatenate([mid[nb - 1 :], mid[: nb - 1]], axis=0) if nb > 1 else mid
        nxt = jnp.concatenate([mid[1:], mid[:1]], axis=0) if nb > 1 else mid
        acc = jnp.dot(prev.reshape(nb * lp, block), table_ref[j, 0], preferred_element_type=jnp.float32, precision=HI)
        acc = acc + jnp.dot(mid.reshape(nb * lp, block), table_ref[j, 1], preferred_element_type=jnp.float32, precision=HI)
        acc = acc + jnp.dot(nxt.reshape(nb * lp, block), table_ref[j, 2], preferred_element_type=jnp.float32, precision=HI)
        dst[j] = acc.reshape(nb, lp, block)

def _merid_rows(src, dst, mir, onehot_ref, w_ref, nb, depth):
    rows, _, lp, block = src.shape
    half = nb // 2
    def mirror_block(b, carry):
        sb = lax.rem(b + half, nb)
        polar = jnp.concatenate([src[pl.ds(0, depth), pl.ds(sb, 1)], src[pl.ds(rows - depth, depth), pl.ds(sb, 1)]], axis=0)
        source = lax.broadcasted_iota(jnp.int32, (block, block), 0)
        onehot = (source == onehot_ref[pl.ds(b, 1), :]).astype(jnp.float32)
        out = jnp.dot(polar.reshape(2 * depth * lp, block), onehot, preferred_element_type=jnp.float32, precision=HI)
        mir[:, pl.ds(b, 1)] = out.reshape(2 * depth, 1, lp, block)
        return carry
    lax.fori_loop(0, nb, mirror_block, 0)
    def row(k):
        if k < 0:
            return mir[-1 - k]
        if k >= rows:
            return mir[depth + (rows - 1 - (k - rows)) - (rows - depth)]
        return src[k]
    for j in range(rows):
        acc = w_ref[0] * src[j]
        for o in range(1, depth + 1):
            acc = acc + w_ref[o] * (row(j - o) + row(j + o))
        dst[j] = acc

def _kernel(order, depth, x_ref, table_ref, onehot_ref, w_ref, o_ref, tmp, mir):
    nb = x_ref.shape[1]
    if order == "zm":
        _zonal_rows(x_ref, tmp, table_ref, nb)
        _merid_rows(tmp, o_ref, mir, onehot_ref, w_ref, nb, depth)
    else:
        _merid_rows(x_ref, tmp, mir, onehot_ref, w_ref, nb, depth)
        _zonal_rows(tmp, o_ref, table_ref, nb)

def level_apply(order, x, table, onehot, merid_w):
    rows, nb, lp, block = x.shape
    depth = merid_w.shape[0] - 1
    vmem = pltpu.MemorySpace.VMEM
    return pl.pallas_call(
        functools.partial(_kernel, order, depth),
        out_shape=jax.ShapeDtypeStruct(x.shape, jnp.float32),
        in_specs=[pl.BlockSpec(memory_space=vmem), pl.BlockSpec(memory_space=vmem), pl.BlockSpec(memory_space=vmem), pl.BlockSpec(memory_space=pltpu.MemorySpace.SMEM)],
        out_specs=pl.BlockSpec(memory_space=vmem),
        scratch_shapes=[pltpu.VMEM(x.shape, jnp.float32), pltpu.VMEM((2 * depth, nb, lp, block), jnp.float32)],
        compiler_params=pltpu.CompilerParams(vmem_limit_bytes=60 * 1024 * 1024),
    )(x, table, onehot, merid_w)


def per_device(gradient, obs_weight, half_width, zonal_coef, mirror_map, merid_coef, vertical_map):
    n_lon = lax.axis_size("lon")
    n_lat = lax.axis_size("lat")
    n_dev = n_lon * n_lat
    lev, rows, cols = gradient.shape
    per = -(-lev // n_dev)
    padded = -(-per // 8) * 8 if per >= 4 else per
    width = zonal_coef.shape[1] - 1
    merid_w = merid_weights(merid_coef)

    def exchange(parts):
        return lax.all_to_all(parts, AXES, 0, 0, tiled=True)

    def col_parts(x):
        x = jnp.pad(x, ((0, n_dev * per - lev), (0, 0), (0, 0)))
        return x.reshape(n_dev, per, rows, cols)

    def to_level(z):
        z = z.reshape(n_lon, n_lat, per, rows, cols).transpose(1, 3, 0, 2, 4)
        z = z.reshape(n_lat * rows, n_lon, per, cols)
        return jnp.pad(z, ((0, 0), (0, 0), (0, padded - per), (0, 0)))

    def level_parts(v):
        v = v[:, :, :per].reshape(n_lat, rows, n_lon, per, cols).transpose(2, 0, 3, 1, 4)
        return v.reshape(n_dev, per, rows, cols)

    def to_column(z):
        return z.reshape(n_dev * per, rows, cols)[:lev]

    def slab(values):
        flat = jnp.zeros((rows * cols,), jnp.float32).at[: values.shape[0]].set(values)
        return jnp.broadcast_to(flat.reshape(1, 1, rows, cols), (n_dev, 1, rows, cols))

    mirror_slab = jnp.zeros((1, 1, rows, cols), jnp.float32).at[0, 0, 0].set(
        mirror_map.astype(jnp.float32)
    )
    zonal_slab = jnp.zeros((1, 1, rows, cols), jnp.float32).at[0, 0, :, : width + 1].set(
        zonal_weights(half_width, zonal_coef)
    )
    got = exchange(
        jnp.concatenate(
            [
                col_parts(gradient),
                jnp.broadcast_to(mirror_slab, (n_dev, 1, rows, cols)),
                jnp.broadcast_to(zonal_slab, (n_dev, 1, rows, cols)),
            ],
            axis=1,
        )
    )
    residual = to_level(got[:, :per])
    mirror_all = (
        got[:, per, 0, :].reshape(n_lon, n_lat, cols)[:, 0].reshape(n_lon * cols).astype(jnp.int32)
    )
    zonal_all = (
        got[:, per + 1, :, : width + 1]
        .reshape(n_lon, n_lat, rows, width + 1)[0]
        .reshape(n_lat * rows, width + 1)
    )
    table = zonal_tables(zonal_all, cols)
    onehot = mirror_tables(mirror_all, cols)

    def forward(x):
        return level_apply("zm", x, table, onehot, merid_w)

    def backward(g):
        return level_apply("mz", g, table, onehot, merid_w)

    def middle(y):
        lifted = jnp.einsum("kl,lji->kji", vertical_map, y, precision=HI)
        return jnp.einsum("lk,lji->kji", vertical_map, obs_weight * lifted, precision=HI)

    def image(x, px_col):
        return x + backward(to_level(exchange(col_parts(middle(px_col)))))

    res_col = gradient
    inc_col = jnp.zeros_like(gradient)
    pres_col = to_column(exchange(level_parts(forward(residual))))
    for outer in range(OUTER):
        last = outer == OUTER - 1
        first = image(residual, pres_col)
        got = exchange(jnp.concatenate([level_parts(forward(first)), level_parts(first)], axis=1))
        pfirst_col = to_column(got[:, :per])
        first_col = to_column(got[:, per:])
        second = image(first, pfirst_col)
        sums = jnp.stack(
            [
                jnp.sum(residual * residual),
                jnp.sum(residual * first),
                jnp.sum(first * first),
                jnp.sum(first * second),
            ]
        )
        parts = [level_parts(second)]
        if not last:
            parts.append(level_parts(forward(second)))
        got = exchange(jnp.concatenate(parts + [slab(sums)], axis=1))
        second_col = to_column(got[:, :per])
        total = jnp.sum(got[:, len(parts) * per, 0, : sums.shape[0]], axis=0)
        sum_rr, sum_rf, sum_ff, sum_fs = total[0], total[1], total[2], total[3]
        determinant = sum_rf * sum_fs - sum_ff * sum_ff
        coef_one = (sum_fs * sum_rr - sum_ff * sum_rf) / determinant
        coef_two = (sum_rf * sum_rf - sum_ff * sum_rr) / determinant
        inc_col = inc_col + coef_one * res_col + coef_two * first_col
        res_col = res_col - coef_one * first_col - coef_two * second_col
        if not last:
            psecond_col = to_column(got[:, per : 2 * per])
            residual = residual - coef_one * first - coef_two * second
            pres_col = pres_col - coef_one * pfirst_col - coef_two * psecond_col
    return (inc_col, res_col)


def solution(mesh):
    placed = (
        P(None, "lat", "lon"),
        P(None, "lat", "lon"),
        P("lat"),
        P("lat", None),
        P("lon"),
        P(),
        P(),
    )
    return jax.shard_map(
        per_device,
        mesh=mesh,
        in_specs=placed,
        out_specs=(P(None, "lat", "lon"), P(None, "lat", "lon")),
        check_vma=False,
    )
```

```python
import functools

import jax
import jax.numpy as jnp
from jax import lax
from jax.experimental import pallas as pl
from jax.experimental.pallas import tpu as pltpu
from jax.sharding import PartitionSpec as P

OUTER = 2
AXES = ("lon", "lat")
HI = lax.Precision.HIGHEST
KERNEL_PRECISION = lax.Precision.HIGH


def zonal_weights(half_width, zonal_coef):
    tap_ids = jnp.arange(zonal_coef.shape[1], dtype=jnp.int32)
    kept = jnp.where(
        tap_ids[None, :] <= half_width[:, None], zonal_coef, jnp.zeros_like(zonal_coef)
    )
    scaling = jnp.sqrt(kept[:, 0] ** 2 + 2.0 * jnp.sum(kept[:, 1:] ** 2, axis=1))
    return kept / scaling[:, None]


def merid_weights(merid_coef):
    norm_value = jnp.sqrt(merid_coef[0] ** 2 + 2.0 * jnp.sum(merid_coef[1:] ** 2))
    return merid_coef / norm_value


def zonal_tables(weights, block):
    width = weights.shape[1] - 1
    positions = jnp.arange(3 * block, dtype=jnp.int32)
    columns = jnp.arange(block, dtype=jnp.int32)
    tap_ids = jnp.arange(width + 1, dtype=jnp.int32)
    distance = jnp.abs(positions[:, None] - block - columns[None, :])
    selector = (distance[:, :, None] == tap_ids[None, None, :]).astype(jnp.float32)
    table = jnp.einsum("pct,jt->jpc", selector, weights, precision=HI)
    return table.reshape(weights.shape[0], 3, block, block)


def mirror_tables(mirror_all, block):
    return (mirror_all % block).reshape(mirror_all.shape[0] // block, block)


def _zonal_rows(src, dst, table_ref, nb):
    rows, _, lp, block = src.shape
    for j in range(rows):
        mid = src[j]
        prev = jnp.concatenate([mid[nb - 1 :], mid[: nb - 1]], axis=0) if nb > 1 else mid
        nxt = jnp.concatenate([mid[1:], mid[:1]], axis=0) if nb > 1 else mid
        acc = jnp.dot(prev.reshape(nb * lp, block), table_ref[j, 0], preferred_element_type=jnp.float32, precision=KERNEL_PRECISION)
        acc = acc + jnp.dot(mid.reshape(nb * lp, block), table_ref[j, 1], preferred_element_type=jnp.float32, precision=KERNEL_PRECISION)
        acc = acc + jnp.dot(nxt.reshape(nb * lp, block), table_ref[j, 2], preferred_element_type=jnp.float32, precision=KERNEL_PRECISION)
        dst[j] = acc.reshape(nb, lp, block)

def _merid_rows(src, dst, mir, onehot_ref, w_ref, nb, depth):
    rows, _, lp, block = src.shape
    half = nb // 2
    def mirror_block(b, carry):
        sb = lax.rem(b + half, nb)
        polar = jnp.concatenate([src[pl.ds(0, depth), pl.ds(sb, 1)], src[pl.ds(rows - depth, depth), pl.ds(sb, 1)]], axis=0)
        source = lax.broadcasted_iota(jnp.int32, (block, block), 0)
        onehot = (source == onehot_ref[pl.ds(b, 1), :]).astype(jnp.float32)
        out = jnp.dot(polar.reshape(2 * depth * lp, block), onehot, preferred_element_type=jnp.float32, precision=KERNEL_PRECISION)
        mir[:, pl.ds(b, 1)] = out.reshape(2 * depth, 1, lp, block)
        return carry
    lax.fori_loop(0, nb, mirror_block, 0)
    def row(k):
        if k < 0:
            return mir[-1 - k]
        if k >= rows:
            return mir[depth + (rows - 1 - (k - rows)) - (rows - depth)]
        return src[k]
    for j in range(rows):
        acc = w_ref[0] * src[j]
        for o in range(1, depth + 1):
            acc = acc + w_ref[o] * (row(j - o) + row(j + o))
        dst[j] = acc

def _kernel(order, depth, x_ref, table_ref, onehot_ref, w_ref, o_ref, tmp, mir):
    nb = x_ref.shape[1]
    if order == "zm":
        _zonal_rows(x_ref, tmp, table_ref, nb)
        _merid_rows(tmp, o_ref, mir, onehot_ref, w_ref, nb, depth)
    else:
        _merid_rows(x_ref, tmp, mir, onehot_ref, w_ref, nb, depth)
        _zonal_rows(tmp, o_ref, table_ref, nb)

def level_apply(order, x, table, onehot, merid_w):
    rows, nb, lp, block = x.shape
    depth = merid_w.shape[0] - 1
    vmem = pltpu.MemorySpace.VMEM
    return pl.pallas_call(
        functools.partial(_kernel, order, depth),
        out_shape=jax.ShapeDtypeStruct(x.shape, jnp.float32),
        in_specs=[pl.BlockSpec(memory_space=vmem), pl.BlockSpec(memory_space=vmem), pl.BlockSpec(memory_space=vmem), pl.BlockSpec(memory_space=pltpu.MemorySpace.SMEM)],
        out_specs=pl.BlockSpec(memory_space=vmem),
        scratch_shapes=[pltpu.VMEM(x.shape, jnp.float32), pltpu.VMEM((2 * depth, nb, lp, block), jnp.float32)],
        compiler_params=pltpu.CompilerParams(vmem_limit_bytes=60 * 1024 * 1024),
    )(x, table, onehot, merid_w)


def per_device(gradient, obs_weight, half_width, zonal_coef, mirror_map, merid_coef, vertical_map):
    n_lon = lax.axis_size("lon")
    n_lat = lax.axis_size("lat")
    n_dev = n_lon * n_lat
    lev, rows, cols = gradient.shape
    per = -(-lev // n_dev)
    padded = -(-per // 8) * 8 if per >= 4 else per
    width = zonal_coef.shape[1] - 1
    merid_w = merid_weights(merid_coef)

    def exchange(parts):
        return lax.all_to_all(parts, AXES, 0, 0, tiled=True)

    def col_parts(x):
        x = jnp.pad(x, ((0, n_dev * per - lev), (0, 0), (0, 0)))
        return x.reshape(n_dev, per, rows, cols)

    def to_level(z):
        z = z.reshape(n_lon, n_lat, per, rows, cols).transpose(1, 3, 0, 2, 4)
        z = z.reshape(n_lat * rows, n_lon, per, cols)
        return jnp.pad(z, ((0, 0), (0, 0), (0, padded - per), (0, 0)))

    def level_parts(v):
        v = v[:, :, :per].reshape(n_lat, rows, n_lon, per, cols).transpose(2, 0, 3, 1, 4)
        return v.reshape(n_dev, per, rows, cols)

    def to_column(z):
        return z.reshape(n_dev * per, rows, cols)[:lev]

    def slab(values):
        flat = jnp.zeros((rows * cols,), jnp.float32).at[: values.shape[0]].set(values)
        return jnp.broadcast_to(flat.reshape(1, 1, rows, cols), (n_dev, 1, rows, cols))

    mirror_slab = jnp.zeros((1, 1, rows, cols), jnp.float32).at[0, 0, 0].set(
        mirror_map.astype(jnp.float32)
    )
    zonal_slab = jnp.zeros((1, 1, rows, cols), jnp.float32).at[0, 0, :, : width + 1].set(
        zonal_weights(half_width, zonal_coef)
    )
    got = exchange(
        jnp.concatenate(
            [
                col_parts(gradient),
                jnp.broadcast_to(mirror_slab, (n_dev, 1, rows, cols)),
                jnp.broadcast_to(zonal_slab, (n_dev, 1, rows, cols)),
            ],
            axis=1,
        )
    )
    residual = to_level(got[:, :per])
    mirror_all = (
        got[:, per, 0, :].reshape(n_lon, n_lat, cols)[:, 0].reshape(n_lon * cols).astype(jnp.int32)
    )
    zonal_all = (
        got[:, per + 1, :, : width + 1]
        .reshape(n_lon, n_lat, rows, width + 1)[0]
        .reshape(n_lat * rows, width + 1)
    )
    table = zonal_tables(zonal_all, cols)
    onehot = mirror_tables(mirror_all, cols)

    def forward(x):
        return level_apply("zm", x, table, onehot, merid_w)

    def backward(g):
        return level_apply("mz", g, table, onehot, merid_w)

    def middle(y):
        lifted = jnp.einsum("kl,lji->kji", vertical_map, y, precision=HI)
        return jnp.einsum("lk,lji->kji", vertical_map, obs_weight * lifted, precision=HI)

    def image(x, px_col):
        return x + backward(to_level(exchange(col_parts(middle(px_col)))))

    res_col = gradient
    inc_col = jnp.zeros_like(gradient)
    pres_col = to_column(exchange(level_parts(forward(residual))))
    for outer in range(OUTER):
        last = outer == OUTER - 1
        first = image(residual, pres_col)
        got = exchange(jnp.concatenate([level_parts(forward(first)), level_parts(first)], axis=1))
        pfirst_col = to_column(got[:, :per])
        first_col = to_column(got[:, per:])
        second = image(first, pfirst_col)
        sums = jnp.stack(
            [
                jnp.sum(residual * residual),
                jnp.sum(residual * first),
                jnp.sum(first * first),
                jnp.sum(first * second),
            ]
        )
        parts = [level_parts(second)]
        if not last:
            parts.append(level_parts(forward(second)))
        got = exchange(jnp.concatenate(parts + [slab(sums)], axis=1))
        second_col = to_column(got[:, :per])
        total = jnp.sum(got[:, len(parts) * per, 0, : sums.shape[0]], axis=0)
        sum_rr, sum_rf, sum_ff, sum_fs = total[0], total[1], total[2], total[3]
        determinant = sum_rf * sum_fs - sum_ff * sum_ff
        coef_one = (sum_fs * sum_rr - sum_ff * sum_rf) / determinant
        coef_two = (sum_rf * sum_rf - sum_ff * sum_rr) / determinant
        inc_col = inc_col + coef_one * res_col + coef_two * first_col
        res_col = res_col - coef_one * first_col - coef_two * second_col
        if not last:
            psecond_col = to_column(got[:, per : 2 * per])
            residual = residual - coef_one * first - coef_two * second
            pres_col = pres_col - coef_one * pfirst_col - coef_two * psecond_col
    return (inc_col, res_col)


def solution(mesh):
    placed = (
        P(None, "lat", "lon"),
        P(None, "lat", "lon"),
        P("lat"),
        P("lat", None),
        P("lon"),
        P(),
        P(),
    )
    return jax.shard_map(
        per_device,
        mesh=mesh,
        in_specs=placed,
        out_specs=(P(None, "lat", "lon"), P(None, "lat", "lon")),
        check_vma=False,
    )
```

```python
import functools

import jax
import jax.numpy as jnp
from jax import lax
from jax.experimental import pallas as pl
from jax.experimental.pallas import tpu as pltpu
from jax.sharding import PartitionSpec as P

OUTER = 2
AXES = ("lon", "lat")
HI = lax.Precision.HIGHEST
KERNEL_PRECISION = lax.Precision.HIGH


def zonal_weights(half_width, zonal_coef):
    tap_ids = jnp.arange(zonal_coef.shape[1], dtype=jnp.int32)
    kept = jnp.where(
        tap_ids[None, :] <= half_width[:, None], zonal_coef, jnp.zeros_like(zonal_coef)
    )
    scaling = jnp.sqrt(kept[:, 0] ** 2 + 2.0 * jnp.sum(kept[:, 1:] ** 2, axis=1))
    return kept / scaling[:, None]


def merid_weights(merid_coef):
    norm_value = jnp.sqrt(merid_coef[0] ** 2 + 2.0 * jnp.sum(merid_coef[1:] ** 2))
    return merid_coef / norm_value


def zonal_tables(weights, block):
    width = weights.shape[1] - 1
    positions = jnp.arange(3 * block, dtype=jnp.int32)
    columns = jnp.arange(block, dtype=jnp.int32)
    tap_ids = jnp.arange(width + 1, dtype=jnp.int32)
    distance = jnp.abs(positions[:, None] - block - columns[None, :])
    selector = (distance[:, :, None] == tap_ids[None, None, :]).astype(jnp.float32)
    table = jnp.einsum("pct,jt->jpc", selector, weights, precision=HI)
    table = table.reshape(weights.shape[0], 3, block, block)
    half = block // 2
    outer = jnp.concatenate([table[:, 2, :half], table[:, 0, half:]], axis=1)
    return jnp.stack([table[:, 1], outer], axis=1)


def mirror_tables(mirror_all, block):
    return (mirror_all % block).reshape(mirror_all.shape[0] // block, block)


def _dot(a, b):
    return jnp.dot(a, b, preferred_element_type=jnp.float32, precision=KERNEL_PRECISION)


def _zonal_rows(src, dst, table_ref, add=None):
    rows, nb, lp, block = src.shape
    lane = lax.broadcasted_iota(jnp.int32, (nb * lp, block), 1)
    for j in range(rows):
        mid = src[j]
        prev = jnp.concatenate([mid[nb - 1 :], mid[: nb - 1]], axis=0) if nb > 1 else mid
        nxt = jnp.concatenate([mid[1:], mid[:1]], axis=0) if nb > 1 else mid
        outer = jnp.where(
            lane >= block // 2, prev.reshape(nb * lp, block), nxt.reshape(nb * lp, block)
        )
        acc = _dot(mid.reshape(nb * lp, block), table_ref[j, 0]) + _dot(outer, table_ref[j, 1])
        acc = acc.reshape(nb, lp, block)
        if add is not None:
            acc = acc + add[j]
        dst[j] = acc


def _merid_rows(src, dst, mir, index_ref, w_ref, depth):
    rows, nb, lp, block = src.shape
    half = nb // 2

    def mirror_block(b, carry):
        sb = lax.rem(b + half, nb)
        polar = jnp.concatenate(
            [src[pl.ds(0, depth), pl.ds(sb, 1)], src[pl.ds(rows - depth, depth), pl.ds(sb, 1)]],
            axis=0,
        )
        source = lax.broadcasted_iota(jnp.int32, (block, block), 0)
        onehot = (source == index_ref[pl.ds(b, 1), :]).astype(jnp.float32)
        out = _dot(polar.reshape(2 * depth * lp, block), onehot)
        mir[:, pl.ds(b, 1)] = out.reshape(2 * depth, 1, lp, block)
        return carry

    lax.fori_loop(0, nb, mirror_block, 0)

    def row(k):
        if k < 0:
            return mir[-1 - k]
        if k >= rows:
            return mir[depth + (rows - 1 - (k - rows)) - (rows - depth)]
        return src[k]

    for j in range(rows):
        acc = w_ref[0] * src[j]
        for o in range(1, depth + 1):
            acc = acc + w_ref[o] * (row(j - o) + row(j + o))
        dst[j] = acc


def _kernel(mode, depth, *refs):
    if mode == "p":
        x_ref, table_ref, index_ref, w_ref, p_ref, tmp, mir = refs
        _zonal_rows(x_ref, tmp, table_ref)
        _merid_rows(tmp, p_ref, mir, index_ref, w_ref, depth)
        return
    a_ref, x_ref, table_ref, index_ref, w_ref = refs[:5]
    if mode == "q":
        f_ref, tmp, mir = refs[5:]
    else:
        f_ref, p_ref, tmp, mir = refs[5:]
    _merid_rows(a_ref, tmp, mir, index_ref, w_ref, depth)
    _zonal_rows(tmp, f_ref, table_ref, add=x_ref)
    if mode == "qp":
        _zonal_rows(f_ref, tmp, table_ref)
        _merid_rows(tmp, p_ref, mir, index_ref, w_ref, depth)


def level_apply(mode, fields, table, index, merid_w):
    shape = fields[0].shape
    rows, nb, lp, block = shape
    depth = merid_w.shape[0] - 1
    vmem = pl.BlockSpec(memory_space=pltpu.MemorySpace.VMEM)
    outs = 2 if mode == "qp" else 1
    result = pl.pallas_call(
        functools.partial(_kernel, mode, depth),
        out_shape=[jax.ShapeDtypeStruct(shape, jnp.float32)] * outs,
        in_specs=[vmem] * (len(fields) + 2) + [pl.BlockSpec(memory_space=pltpu.MemorySpace.SMEM)],
        out_specs=[vmem] * outs,
        scratch_shapes=[
            pltpu.VMEM(shape, jnp.float32),
            pltpu.VMEM((2 * depth, nb, lp, block), jnp.float32),
        ],
        compiler_params=pltpu.CompilerParams(vmem_limit_bytes=60 * 1024 * 1024),
    )(*fields, table, index, merid_w)
    return result if outs == 2 else result[0]


def per_device(gradient, obs_weight, half_width, zonal_coef, mirror_map, merid_coef, vertical_map):
    n_lon = lax.axis_size("lon")
    n_lat = lax.axis_size("lat")
    n_dev = n_lon * n_lat
    lev, rows, cols = gradient.shape
    per = -(-lev // n_dev)
    padded = -(-per // 8) * 8 if per >= 4 else per
    width = zonal_coef.shape[1] - 1
    merid_w = merid_weights(merid_coef)

    def exchange(parts):
        return lax.all_to_all(parts, AXES, 0, 0, tiled=True)

    def col_parts(x):
        x = jnp.pad(x, ((0, n_dev * per - lev), (0, 0), (0, 0)))
        return x.reshape(n_dev, per, rows, cols)

    def to_level(z):
        z = z.reshape(n_lon, n_lat, per, rows, cols).transpose(1, 3, 0, 2, 4)
        z = z.reshape(n_lat * rows, n_lon, per, cols)
        return jnp.pad(z, ((0, 0), (0, 0), (0, padded - per), (0, 0)))

    def level_parts(v):
        v = v[:, :, :per].reshape(n_lat, rows, n_lon, per, cols).transpose(2, 0, 3, 1, 4)
        return v.reshape(n_dev, per, rows, cols)

    def to_column(z):
        return z.reshape(n_dev * per, rows, cols)[:lev]

    def slab(values):
        flat = jnp.zeros((rows * cols,), jnp.float32).at[: values.shape[0]].set(values)
        return jnp.broadcast_to(flat.reshape(1, 1, rows, cols), (n_dev, 1, rows, cols))

    mirror_slab = jnp.zeros((1, 1, rows, cols), jnp.float32).at[0, 0, 0].set(
        mirror_map.astype(jnp.float32)
    )
    zonal_slab = jnp.zeros((1, 1, rows, cols), jnp.float32).at[0, 0, :, : width + 1].set(
        zonal_weights(half_width, zonal_coef)
    )
    got = exchange(
        jnp.concatenate(
            [
                col_parts(gradient),
                jnp.broadcast_to(mirror_slab, (n_dev, 1, rows, cols)),
                jnp.broadcast_to(zonal_slab, (n_dev, 1, rows, cols)),
            ],
            axis=1,
        )
    )
    residual = to_level(got[:, :per])
    mirror_all = (
        got[:, per, 0, :].reshape(n_lon, n_lat, cols)[:, 0].reshape(n_lon * cols).astype(jnp.int32)
    )
    zonal_all = (
        got[:, per + 1, :, : width + 1]
        .reshape(n_lon, n_lat, rows, width + 1)[0]
        .reshape(n_lat * rows, width + 1)
    )
    table = zonal_tables(zonal_all, cols)
    onehot = mirror_tables(mirror_all, cols)

    def forward(x):
        return level_apply("p", (x,), table, onehot, merid_w)

    def middle(y):
        lifted = jnp.einsum("kl,lji->kji", vertical_map, y, precision=HI)
        return jnp.einsum("lk,lji->kji", vertical_map, obs_weight * lifted, precision=HI)

    def image(x, px_col, mode):
        return level_apply(mode, (to_level(exchange(col_parts(middle(px_col)))), x), table, onehot, merid_w)

    res_col = gradient
    inc_col = jnp.zeros_like(gradient)
    pres_col = to_column(exchange(level_parts(forward(residual))))
    for outer in range(OUTER):
        last = outer == OUTER - 1
        first, pfirst = image(residual, pres_col, "qp")
        got = exchange(jnp.concatenate([level_parts(pfirst), level_parts(first)], axis=1))
        pfirst_col = to_column(got[:, :per])
        first_col = to_column(got[:, per:])
        if last:
            second = image(first, pfirst_col, "q")
        else:
            second, psecond = image(first, pfirst_col, "qp")
        sums = jnp.stack(
            [
                jnp.sum(residual * residual),
                jnp.sum(residual * first),
                jnp.sum(first * first),
                jnp.sum(first * second),
            ]
        )
        parts = [level_parts(second)]
        if not last:
            parts.append(level_parts(psecond))
        got = exchange(jnp.concatenate(parts + [slab(sums)], axis=1))
        second_col = to_column(got[:, :per])
        total = jnp.sum(got[:, len(parts) * per, 0, : sums.shape[0]], axis=0)
        sum_rr, sum_rf, sum_ff, sum_fs = total[0], total[1], total[2], total[3]
        determinant = sum_rf * sum_fs - sum_ff * sum_ff
        coef_one = (sum_fs * sum_rr - sum_ff * sum_rf) / determinant
        coef_two = (sum_rf * sum_rf - sum_ff * sum_rr) / determinant
        inc_col = inc_col + coef_one * res_col + coef_two * first_col
        res_col = res_col - coef_one * first_col - coef_two * second_col
        if not last:
            psecond_col = to_column(got[:, per : 2 * per])
            residual = residual - coef_one * first - coef_two * second
            pres_col = pres_col - coef_one * pfirst_col - coef_two * psecond_col
    return (inc_col, res_col)


def solution(mesh):
    placed = (
        P(None, "lat", "lon"),
        P(None, "lat", "lon"),
        P("lat"),
        P("lat", None),
        P("lon"),
        P(),
        P(),
    )
    return jax.shard_map(
        per_device,
        mesh=mesh,
        in_specs=placed,
        out_specs=(P(None, "lat", "lon"), P(None, "lat", "lon")),
        check_vma=False,
    )
```

```python
import functools

import jax
import jax.numpy as jnp
from jax import lax
from jax.experimental import pallas as pl
from jax.experimental.pallas import tpu as pltpu
from jax.sharding import PartitionSpec as P

OUTER = 2
AXES = ("lon", "lat")
HI = lax.Precision.HIGHEST
KERNEL_PRECISION = lax.Precision.HIGH


def zonal_weights(half_width, zonal_coef):
    tap_ids = jnp.arange(zonal_coef.shape[1], dtype=jnp.int32)
    kept = jnp.where(
        tap_ids[None, :] <= half_width[:, None], zonal_coef, jnp.zeros_like(zonal_coef)
    )
    scaling = jnp.sqrt(kept[:, 0] ** 2 + 2.0 * jnp.sum(kept[:, 1:] ** 2, axis=1))
    return kept / scaling[:, None]


def merid_weights(merid_coef):
    norm_value = jnp.sqrt(merid_coef[0] ** 2 + 2.0 * jnp.sum(merid_coef[1:] ** 2))
    return merid_coef / norm_value


def zonal_tables(weights, block):
    width = weights.shape[1] - 1
    positions = jnp.arange(3 * block, dtype=jnp.int32)
    columns = jnp.arange(block, dtype=jnp.int32)
    tap_ids = jnp.arange(width + 1, dtype=jnp.int32)
    distance = jnp.abs(positions[:, None] - block - columns[None, :])
    selector = (distance[:, :, None] == tap_ids[None, None, :]).astype(jnp.float32)
    table = jnp.einsum("pct,jt->jpc", selector, weights, precision=HI)
    table = table.reshape(weights.shape[0], 3, block, block)
    half = block // 2
    outer = jnp.concatenate([table[:, 2, :half], table[:, 0, half:]], axis=1)
    return jnp.stack([table[:, 1], outer], axis=1)


def mirror_tables(mirror_all, block):
    return (mirror_all % block).reshape(mirror_all.shape[0] // block, block)


def _dot(a, b):
    return jnp.dot(a, b, preferred_element_type=jnp.float32, precision=KERNEL_PRECISION)


def _zonal_rows(src, dst, table_ref, add=None):
    rows, nb, lp, block = src.shape
    lane = lax.broadcasted_iota(jnp.int32, (nb * lp, block), 1)
    for j in range(rows):
        mid = src[j]
        prev = jnp.concatenate([mid[nb - 1 :], mid[: nb - 1]], axis=0) if nb > 1 else mid
        nxt = jnp.concatenate([mid[1:], mid[:1]], axis=0) if nb > 1 else mid
        outer = jnp.where(
            lane >= block // 2, prev.reshape(nb * lp, block), nxt.reshape(nb * lp, block)
        )
        acc = _dot(mid.reshape(nb * lp, block), table_ref[j, 0]) + _dot(outer, table_ref[j, 1])
        acc = acc.reshape(nb, lp, block)
        if add is not None:
            acc = acc + add[j]
        dst[j] = acc


def _merid_rows(src, dst, mir, index_ref, w_ref, depth):
    rows, nb, lp, block = src.shape
    half = nb // 2

    def mirror_block(b, carry):
        sb = lax.rem(b + half, nb)
        polar = jnp.concatenate(
            [src[pl.ds(0, depth), pl.ds(sb, 1)], src[pl.ds(rows - depth, depth), pl.ds(sb, 1)]],
            axis=0,
        )
        source = lax.broadcasted_iota(jnp.int32, (block, block), 0)
        onehot = (source == index_ref[pl.ds(b, 1), :]).astype(jnp.float32)
        out = _dot(polar.reshape(2 * depth * lp, block), onehot)
        mir[:, pl.ds(b, 1)] = out.reshape(2 * depth, 1, lp, block)
        return carry

    lax.fori_loop(0, nb, mirror_block, 0)

    def row(k):
        if k < 0:
            return mir[-1 - k]
        if k >= rows:
            return mir[depth + (rows - 1 - (k - rows)) - (rows - depth)]
        return src[k]

    for j in range(rows):
        acc = w_ref[0] * src[j]
        for o in range(1, depth + 1):
            acc = acc + w_ref[o] * (row(j - o) + row(j + o))
        dst[j] = acc


def _kernel(mode, depth, *refs):
    if mode == "p":
        x_ref, table_ref, index_ref, w_ref, p_ref, tmp, mir = refs
        _zonal_rows(x_ref, tmp, table_ref)
        _merid_rows(tmp, p_ref, mir, index_ref, w_ref, depth)
        return
    a_ref, x_ref, table_ref, index_ref, w_ref = refs[:5]
    if mode == "q":
        f_ref, tmp, mir = refs[5:]
    else:
        f_ref, p_ref, tmp, mir = refs[5:]
    _merid_rows(a_ref, tmp, mir, index_ref, w_ref, depth)
    _zonal_rows(tmp, f_ref, table_ref, add=x_ref)
    if mode == "qp":
        _zonal_rows(f_ref, tmp, table_ref)
        _merid_rows(tmp, p_ref, mir, index_ref, w_ref, depth)


def level_apply(mode, fields, table, index, merid_w):
    shape = fields[0].shape
    rows, nb, lp, block = shape
    depth = merid_w.shape[0] - 1
    vmem = pl.BlockSpec(memory_space=pltpu.MemorySpace.VMEM)
    outs = 2 if mode == "qp" else 1
    result = pl.pallas_call(
        functools.partial(_kernel, mode, depth),
        out_shape=[jax.ShapeDtypeStruct(shape, jnp.float32)] * outs,
        in_specs=[vmem] * (len(fields) + 2) + [pl.BlockSpec(memory_space=pltpu.MemorySpace.SMEM)],
        out_specs=[vmem] * outs,
        scratch_shapes=[
            pltpu.VMEM(shape, jnp.float32),
            pltpu.VMEM((2 * depth, nb, lp, block), jnp.float32),
        ],
        compiler_params=pltpu.CompilerParams(vmem_limit_bytes=60 * 1024 * 1024),
    )(*fields, table, index, merid_w)
    return result if outs == 2 else result[0]


def per_device(gradient, obs_weight, half_width, zonal_coef, mirror_map, merid_coef, vertical_map):
    n_lon = lax.axis_size("lon")
    n_lat = lax.axis_size("lat")
    n_dev = n_lon * n_lat
    lev, rows, cols = gradient.shape
    per = -(-lev // n_dev)
    padded = -(-per // 8) * 8 if per >= 4 else per
    width = zonal_coef.shape[1] - 1
    merid_w = merid_weights(merid_coef)

    def exchange(parts):
        return lax.all_to_all(parts, AXES, 0, 0, tiled=True)

    def col_parts(x):
        x = jnp.pad(x, ((0, n_dev * per - lev), (0, 0), (0, 0)))
        return x.reshape(n_dev, per, rows, cols)

    def to_level(z):
        z = z.reshape(n_lon, n_lat, per, rows, cols).transpose(1, 3, 0, 2, 4)
        z = z.reshape(n_lat * rows, n_lon, per, cols)
        return jnp.pad(z, ((0, 0), (0, 0), (0, padded - per), (0, 0)))

    def level_parts(v):
        v = v[:, :, :per].reshape(n_lat, rows, n_lon, per, cols).transpose(2, 0, 3, 1, 4)
        return v.reshape(n_dev, per, rows, cols)

    def to_column(z):
        return z.reshape(n_dev * per, rows, cols)[:lev]

    lanes = cols if rows >= 4 else 1

    def slab(values):
        flat = jnp.repeat(values, lanes)
        flat = jnp.zeros((rows * cols,), jnp.float32).at[: flat.shape[0]].set(flat)
        return jnp.broadcast_to(flat.reshape(1, 1, rows, cols), (n_dev, 1, rows, cols))

    def totals(piece):
        flat = piece.reshape(n_dev, rows * cols)[:, : 4 * lanes].reshape(n_dev, 4, lanes)
        return jnp.sum(flat, axis=0)

    mirror_slab = jnp.zeros((1, 1, rows, cols), jnp.float32).at[0, 0, 0].set(
        mirror_map.astype(jnp.float32)
    )
    zonal_slab = jnp.zeros((1, 1, rows, cols), jnp.float32).at[0, 0, :, : width + 1].set(
        zonal_weights(half_width, zonal_coef)
    )
    got = exchange(
        jnp.concatenate(
            [
                col_parts(gradient),
                jnp.broadcast_to(mirror_slab, (n_dev, 1, rows, cols)),
                jnp.broadcast_to(zonal_slab, (n_dev, 1, rows, cols)),
            ],
            axis=1,
        )
    )
    residual = to_level(got[:, :per])
    mirror_all = (
        got[:, per, 0, :].reshape(n_lon, n_lat, cols)[:, 0].reshape(n_lon * cols).astype(jnp.int32)
    )
    zonal_all = (
        got[:, per + 1, :, : width + 1]
        .reshape(n_lon, n_lat, rows, width + 1)[0]
        .reshape(n_lat * rows, width + 1)
    )
    table = zonal_tables(zonal_all, cols)
    onehot = mirror_tables(mirror_all, cols)

    def forward(x):
        return level_apply("p", (x,), table, onehot, merid_w)

    def middle(y):
        lifted = jnp.einsum("kl,lji->kji", vertical_map, y, precision=HI)
        return jnp.einsum("lk,lji->kji", vertical_map, obs_weight * lifted, precision=HI)

    def image(x, px_col, mode):
        return level_apply(mode, (to_level(exchange(col_parts(middle(px_col)))), x), table, onehot, merid_w)

    res_col = gradient
    inc_col = jnp.zeros_like(gradient)
    pres_col = to_column(exchange(level_parts(forward(residual))))
    for outer in range(OUTER):
        last = outer == OUTER - 1
        first, pfirst = image(residual, pres_col, "qp")
        got = exchange(jnp.concatenate([level_parts(pfirst), level_parts(first)], axis=1))
        pfirst_col = to_column(got[:, :per])
        first_col = to_column(got[:, per:])
        if last:
            second = image(first, pfirst_col, "q")
        else:
            second, psecond = image(first, pfirst_col, "qp")
        sums = jnp.stack(
            [
                jnp.sum(residual * residual),
                jnp.sum(residual * first),
                jnp.sum(first * first),
                jnp.sum(first * second),
            ]
        )
        parts = [level_parts(second)]
        if not last:
            parts.append(level_parts(psecond))
        got = exchange(jnp.concatenate(parts + [slab(sums)], axis=1))
        second_col = to_column(got[:, :per])
        total = totals(got[:, len(parts) * per])
        sum_rr, sum_rf, sum_ff, sum_fs = total[0], total[1], total[2], total[3]
        determinant = sum_rf * sum_fs - sum_ff * sum_ff
        coef_one = (sum_fs * sum_rr - sum_ff * sum_rf) / determinant
        coef_two = (sum_rf * sum_rf - sum_ff * sum_rr) / determinant
        inc_col = inc_col + coef_one * res_col + coef_two * first_col
        res_col = res_col - coef_one * first_col - coef_two * second_col
        if not last:
            psecond_col = to_column(got[:, per : 2 * per])
            residual = residual - coef_one * first - coef_two * second
            pres_col = pres_col - coef_one * pfirst_col - coef_two * psecond_col
    return (inc_col, res_col)


def solution(mesh):
    placed = (
        P(None, "lat", "lon"),
        P(None, "lat", "lon"),
        P("lat"),
        P("lat", None),
        P("lon"),
        P(),
        P(),
    )
    return jax.shard_map(
        per_device,
        mesh=mesh,
        in_specs=placed,
        out_specs=(P(None, "lat", "lon"), P(None, "lat", "lon")),
        check_vma=False,
    )
```

```python
import functools

import jax
import jax.numpy as jnp
from jax import lax
from jax.experimental import pallas as pl
from jax.experimental.pallas import tpu as pltpu
from jax.sharding import PartitionSpec as P

OUTER = 2
AXES = ("lon", "lat")
HI = lax.Precision.HIGHEST
KERNEL_PRECISION = lax.Precision.HIGH


def zonal_weights(half_width, zonal_coef):
    tap_ids = jnp.arange(zonal_coef.shape[1], dtype=jnp.int32)
    kept = jnp.where(
        tap_ids[None, :] <= half_width[:, None], zonal_coef, jnp.zeros_like(zonal_coef)
    )
    scaling = jnp.sqrt(kept[:, 0] ** 2 + 2.0 * jnp.sum(kept[:, 1:] ** 2, axis=1))
    return kept / scaling[:, None]


def merid_weights(merid_coef):
    norm_value = jnp.sqrt(merid_coef[0] ** 2 + 2.0 * jnp.sum(merid_coef[1:] ** 2))
    return merid_coef / norm_value


def zonal_tables(weights, block):
    width = weights.shape[1] - 1
    positions = jnp.arange(3 * block, dtype=jnp.int32)
    columns = jnp.arange(block, dtype=jnp.int32)
    tap_ids = jnp.arange(width + 1, dtype=jnp.int32)
    distance = jnp.abs(positions[:, None] - block - columns[None, :])
    selector = (distance[:, :, None] == tap_ids[None, None, :]).astype(jnp.float32)
    table = jnp.einsum("pct,jt->jpc", selector, weights, precision=HI)
    table = table.reshape(weights.shape[0], 3, block, block)
    half = block // 2
    outer = jnp.concatenate([table[:, 2, :half], table[:, 0, half:]], axis=1)
    return jnp.stack([table[:, 1], outer], axis=1)


def mirror_tables(mirror_all, block):
    return (mirror_all % block).reshape(mirror_all.shape[0] // block, block)


def _dot(a, b):
    return jnp.dot(a, b, preferred_element_type=jnp.float32, precision=KERNEL_PRECISION)


def _zonal_rows(src, dst, table_ref, add=None):
    rows, nb, lp, block = src.shape
    lane = lax.broadcasted_iota(jnp.int32, (nb * lp, block), 1)
    for j in range(rows):
        mid = src[j]
        prev = jnp.concatenate([mid[nb - 1 :], mid[: nb - 1]], axis=0) if nb > 1 else mid
        nxt = jnp.concatenate([mid[1:], mid[:1]], axis=0) if nb > 1 else mid
        outer = jnp.where(
            lane >= block // 2, prev.reshape(nb * lp, block), nxt.reshape(nb * lp, block)
        )
        acc = _dot(mid.reshape(nb * lp, block), table_ref[j, 0]) + _dot(outer, table_ref[j, 1])
        acc = acc.reshape(nb, lp, block)
        if add is not None:
            acc = acc + add[j]
        dst[j] = acc


def _merid_rows(src, dst, mir, index_ref, w_ref, depth):
    rows, nb, lp, block = src.shape
    half = nb // 2

    def mirror_block(b, carry):
        sb = lax.rem(b + half, nb)
        polar = jnp.concatenate(
            [src[pl.ds(0, depth), pl.ds(sb, 1)], src[pl.ds(rows - depth, depth), pl.ds(sb, 1)]],
            axis=0,
        )
        source = lax.broadcasted_iota(jnp.int32, (block, block), 0)
        onehot = (source == index_ref[pl.ds(b, 1), :]).astype(jnp.float32)
        out = _dot(polar.reshape(2 * depth * lp, block), onehot)
        mir[:, pl.ds(b, 1)] = out.reshape(2 * depth, 1, lp, block)
        return carry

    lax.fori_loop(0, nb, mirror_block, 0)

    def row(k):
        if k < 0:
            return mir[-1 - k]
        if k >= rows:
            return mir[depth + (rows - 1 - (k - rows)) - (rows - depth)]
        return src[k]

    for j in range(rows):
        acc = w_ref[0] * src[j]
        for o in range(1, depth + 1):
            acc = acc + w_ref[o] * (row(j - o) + row(j + o))
        dst[j] = acc


def _unpack(parts_ref, dst, n_lat):
    _, per, rl, _ = parts_ref.shape
    nb = dst.shape[1]

    def one_block(b, carry):
        for a in range(n_lat):
            for lev in range(per):
                tile = parts_ref[b * n_lat + a, lev]
                for r in range(rl):
                    dst[a * rl + r, pl.ds(b, 1), pl.ds(lev, 1), :] = tile[r : r + 1].reshape(1, 1, -1)
        return carry

    lax.fori_loop(0, nb, one_block, 0)


def _pack(src, parts_ref, n_lat):
    _, per, rl, _ = parts_ref.shape
    nb = src.shape[1]

    def one_block(b, carry):
        for a in range(n_lat):
            for lev in range(per):
                tile = jnp.concatenate(
                    [src[a * rl + r, pl.ds(b, 1), pl.ds(lev, 1), :].reshape(1, -1) for r in range(rl)],
                    axis=0,
                )
                parts_ref[b * n_lat + a, lev] = tile
        return carry

    lax.fori_loop(0, nb, one_block, 0)


def _kernel(mode, depth, n_lat, *refs):
    if mode == "p":
        x_ref, table_ref, index_ref, w_ref, p_ref, u, v, mir = refs
        _unpack(x_ref, u, n_lat)
        _zonal_rows(u, v, table_ref)
        _merid_rows(v, u, mir, index_ref, w_ref, depth)
        _pack(u, p_ref, n_lat)
        return
    a_ref, x_ref, table_ref, index_ref, w_ref = refs[:5]
    if mode == "q":
        f_ref, u, v, mir = refs[5:]
    else:
        f_ref, p_ref, u, v, mir = refs[5:]
    _unpack(a_ref, u, n_lat)
    _merid_rows(u, v, mir, index_ref, w_ref, depth)
    _unpack(x_ref, u, n_lat)
    _zonal_rows(v, v, table_ref, add=u)
    _pack(v, f_ref, n_lat)
    if mode == "qp":
        _zonal_rows(v, u, table_ref)
        _merid_rows(u, v, mir, index_ref, w_ref, depth)
        _pack(v, p_ref, n_lat)


def level_apply(mode, fields, table, index, merid_w, n_lat, padded):
    shape = fields[0].shape
    n_dev, per, rl, block = shape
    nb = n_dev // n_lat
    level_shape = (n_lat * rl, nb, padded, block)
    depth = merid_w.shape[0] - 1
    vmem = pl.BlockSpec(memory_space=pltpu.MemorySpace.VMEM)
    outs = 2 if mode == "qp" else 1
    result = pl.pallas_call(
        functools.partial(_kernel, mode, depth, n_lat),
        out_shape=[jax.ShapeDtypeStruct(shape, jnp.float32)] * outs,
        in_specs=[vmem] * (len(fields) + 2) + [pl.BlockSpec(memory_space=pltpu.MemorySpace.SMEM)],
        out_specs=[vmem] * outs,
        scratch_shapes=[
            pltpu.VMEM(level_shape, jnp.float32),
            pltpu.VMEM(level_shape, jnp.float32),
            pltpu.VMEM((2 * depth, nb, padded, block), jnp.float32),
        ],
        compiler_params=pltpu.CompilerParams(vmem_limit_bytes=60 * 1024 * 1024),
    )(*fields, table, index, merid_w)
    return result if outs == 2 else result[0]


def per_device(gradient, obs_weight, half_width, zonal_coef, mirror_map, merid_coef, vertical_map):
    n_lon = lax.axis_size("lon")
    n_lat = lax.axis_size("lat")
    n_dev = n_lon * n_lat
    lev, rows, cols = gradient.shape
    per = -(-lev // n_dev)
    padded = -(-per // 8) * 8 if per >= 4 else per
    width = zonal_coef.shape[1] - 1
    merid_w = merid_weights(merid_coef)

    def exchange(parts):
        return lax.all_to_all(parts, AXES, 0, 0, tiled=True)

    def col_parts(x):
        x = jnp.pad(x, ((0, n_dev * per - lev), (0, 0), (0, 0)))
        return x.reshape(n_dev, per, rows, cols)

    def to_column(z):
        return z.reshape(n_dev * per, rows, cols)[:lev]

    lanes = cols if rows >= 4 else 1

    def slab(values):
        flat = jnp.repeat(values, lanes)
        flat = jnp.zeros((rows * cols,), jnp.float32).at[: flat.shape[0]].set(flat)
        return jnp.broadcast_to(flat.reshape(1, 1, rows, cols), (n_dev, 1, rows, cols))

    def totals(piece):
        flat = piece.reshape(n_dev, rows * cols)[:, : 4 * lanes].reshape(n_dev, 4, lanes)
        return jnp.sum(flat, axis=0)

    mirror_slab = jnp.zeros((1, 1, rows, cols), jnp.float32).at[0, 0, 0].set(
        mirror_map.astype(jnp.float32)
    )
    zonal_slab = jnp.zeros((1, 1, rows, cols), jnp.float32).at[0, 0, :, : width + 1].set(
        zonal_weights(half_width, zonal_coef)
    )
    got = exchange(
        jnp.concatenate(
            [
                col_parts(gradient),
                jnp.broadcast_to(mirror_slab, (n_dev, 1, rows, cols)),
                jnp.broadcast_to(zonal_slab, (n_dev, 1, rows, cols)),
            ],
            axis=1,
        )
    )
    residual = got[:, :per]
    mirror_all = (
        got[:, per, 0, :].reshape(n_lon, n_lat, cols)[:, 0].reshape(n_lon * cols).astype(jnp.int32)
    )
    zonal_all = (
        got[:, per + 1, :, : width + 1]
        .reshape(n_lon, n_lat, rows, width + 1)[0]
        .reshape(n_lat * rows, width + 1)
    )
    table = zonal_tables(zonal_all, cols)
    onehot = mirror_tables(mirror_all, cols)

    def forward(x):
        return level_apply("p", (x,), table, onehot, merid_w, n_lat, padded)

    def middle(y):
        lifted = jnp.einsum("kl,lji->kji", vertical_map, y, precision=HI)
        return jnp.einsum("lk,lji->kji", vertical_map, obs_weight * lifted, precision=HI)

    def image(x, px_col, mode):
        return level_apply(
            mode, (exchange(col_parts(middle(px_col))), x), table, onehot, merid_w, n_lat, padded
        )

    res_col = gradient
    inc_col = jnp.zeros_like(gradient)
    pres_col = to_column(exchange(forward(residual)))
    for outer in range(OUTER):
        last = outer == OUTER - 1
        first, pfirst = image(residual, pres_col, "qp")
        got = exchange(jnp.concatenate([pfirst, first], axis=1))
        pfirst_col = to_column(got[:, :per])
        first_col = to_column(got[:, per:])
        if last:
            second = image(first, pfirst_col, "q")
        else:
            second, psecond = image(first, pfirst_col, "qp")
        sums = jnp.stack(
            [
                jnp.sum(residual * residual),
                jnp.sum(residual * first),
                jnp.sum(first * first),
                jnp.sum(first * second),
            ]
        )
        parts = [(second)]
        if not last:
            parts.append((psecond))
        got = exchange(jnp.concatenate(parts + [slab(sums)], axis=1))
        second_col = to_column(got[:, :per])
        total = totals(got[:, len(parts) * per])
        sum_rr, sum_rf, sum_ff, sum_fs = total[0], total[1], total[2], total[3]
        determinant = sum_rf * sum_fs - sum_ff * sum_ff
        coef_one = (sum_fs * sum_rr - sum_ff * sum_rf) / determinant
        coef_two = (sum_rf * sum_rf - sum_ff * sum_rr) / determinant
        inc_col = inc_col + coef_one * res_col + coef_two * first_col
        res_col = res_col - coef_one * first_col - coef_two * second_col
        if not last:
            psecond_col = to_column(got[:, per : 2 * per])
            residual = residual - coef_one * first - coef_two * second
            pres_col = pres_col - coef_one * pfirst_col - coef_two * psecond_col
    return (inc_col, res_col)


def solution(mesh):
    placed = (
        P(None, "lat", "lon"),
        P(None, "lat", "lon"),
        P("lat"),
        P("lat", None),
        P("lon"),
        P(),
        P(),
    )
    return jax.shard_map(
        per_device,
        mesh=mesh,
        in_specs=placed,
        out_specs=(P(None, "lat", "lon"), P(None, "lat", "lon")),
        check_vma=False,
    )
```

```python
import functools

import jax
import jax.numpy as jnp
from jax import lax
from jax.experimental import pallas as pl
from jax.experimental.pallas import tpu as pltpu
from jax.sharding import PartitionSpec as P

OUTER = 2
AXES = ("lon", "lat")
HI = lax.Precision.HIGHEST
KERNEL_PRECISION = lax.Precision.HIGH


def zonal_weights(half_width, zonal_coef):
    tap_ids = jnp.arange(zonal_coef.shape[1], dtype=jnp.int32)
    kept = jnp.where(
        tap_ids[None, :] <= half_width[:, None], zonal_coef, jnp.zeros_like(zonal_coef)
    )
    scaling = jnp.sqrt(kept[:, 0] ** 2 + 2.0 * jnp.sum(kept[:, 1:] ** 2, axis=1))
    return kept / scaling[:, None]


def merid_weights(merid_coef):
    norm_value = jnp.sqrt(merid_coef[0] ** 2 + 2.0 * jnp.sum(merid_coef[1:] ** 2))
    return merid_coef / norm_value


def zonal_tables(weights, block):
    width = weights.shape[1] - 1
    positions = jnp.arange(3 * block, dtype=jnp.int32)
    columns = jnp.arange(block, dtype=jnp.int32)
    tap_ids = jnp.arange(width + 1, dtype=jnp.int32)
    distance = jnp.abs(positions[:, None] - block - columns[None, :])
    selector = (distance[:, :, None] == tap_ids[None, None, :]).astype(jnp.float32)
    table = jnp.einsum("pct,jt->jpc", selector, weights, precision=HI)
    table = table.reshape(weights.shape[0], 3, block, block)
    half = block // 2
    outer = jnp.concatenate([table[:, 2, :half], table[:, 0, half:]], axis=1)
    return jnp.stack([table[:, 1], outer], axis=1)


def mirror_tables(mirror_all, block):
    return (mirror_all % block).reshape(mirror_all.shape[0] // block, block)


def _dot(a, b):
    return jnp.dot(a, b, preferred_element_type=jnp.float32, precision=KERNEL_PRECISION)


def _zonal_rows(src, dst, table_ref, add=None):
    rows, nb, lp, block = src.shape
    lane = lax.broadcasted_iota(jnp.int32, (nb * lp, block), 1)
    for j in range(rows):
        mid = src[j]
        prev = jnp.concatenate([mid[nb - 1 :], mid[: nb - 1]], axis=0) if nb > 1 else mid
        nxt = jnp.concatenate([mid[1:], mid[:1]], axis=0) if nb > 1 else mid
        outer = jnp.where(
            lane >= block // 2, prev.reshape(nb * lp, block), nxt.reshape(nb * lp, block)
        )
        acc = _dot(mid.reshape(nb * lp, block), table_ref[j, 0]) + _dot(outer, table_ref[j, 1])
        acc = acc.reshape(nb, lp, block)
        if add is not None:
            acc = acc + add[j]
        dst[j] = acc


def _merid_rows(src, dst, mir, index_ref, w_ref, depth):
    rows, nb, lp, block = src.shape
    half = nb // 2

    def mirror_block(b, carry):
        sb = lax.rem(b + half, nb)
        polar = jnp.concatenate(
            [src[pl.ds(0, depth), pl.ds(sb, 1)], src[pl.ds(rows - depth, depth), pl.ds(sb, 1)]],
            axis=0,
        )
        source = lax.broadcasted_iota(jnp.int32, (block, block), 0)
        onehot = (source == index_ref[pl.ds(b, 1), :]).astype(jnp.float32)
        out = _dot(polar.reshape(2 * depth * lp, block), onehot)
        mir[:, pl.ds(b, 1)] = out.reshape(2 * depth, 1, lp, block)
        return carry

    lax.fori_loop(0, nb, mirror_block, 0)

    def row(k):
        if k < 0:
            return mir[-1 - k]
        if k >= rows:
            return mir[depth + (rows - 1 - (k - rows)) - (rows - depth)]
        return src[k]

    for j in range(rows):
        acc = w_ref[0] * src[j]
        for o in range(1, depth + 1):
            acc = acc + w_ref[o] * (row(j - o) + row(j + o))
        dst[j] = acc


def _unpack(parts_ref, dst, n_lat):
    _, per, rl, _ = parts_ref.shape
    nb = dst.shape[1]

    def one_block(b, carry):
        for a in range(n_lat):
            for lev in range(per):
                tile = parts_ref[b * n_lat + a, lev]
                for r in range(rl):
                    dst[a * rl + r, pl.ds(b, 1), pl.ds(lev, 1), :] = tile[r : r + 1].reshape(1, 1, -1)
        return carry

    lax.fori_loop(0, nb, one_block, 0)


def _pack(src, parts_ref, n_lat):
    _, per, rl, _ = parts_ref.shape
    nb = src.shape[1]

    def one_block(b, carry):
        for a in range(n_lat):
            for lev in range(per):
                tile = jnp.concatenate(
                    [src[a * rl + r, pl.ds(b, 1), pl.ds(lev, 1), :].reshape(1, -1) for r in range(rl)],
                    axis=0,
                )
                parts_ref[b * n_lat + a, lev] = tile
        return carry

    lax.fori_loop(0, nb, one_block, 0)


def _kernel(mode, depth, n_lat, *refs):
    if mode == "p":
        x_ref, table_ref, index_ref, w_ref, p_ref, u, v, mir = refs
        _unpack(x_ref, u, n_lat)
        _zonal_rows(u, v, table_ref)
        _merid_rows(v, u, mir, index_ref, w_ref, depth)
        _pack(u, p_ref, n_lat)
        return
    a_ref, x_ref, table_ref, index_ref, w_ref = refs[:5]
    if mode == "q":
        f_ref, u, v, mir = refs[5:]
    else:
        f_ref, p_ref, u, v, mir = refs[5:]
    _unpack(a_ref, u, n_lat)
    _merid_rows(u, v, mir, index_ref, w_ref, depth)
    _unpack(x_ref, u, n_lat)
    _zonal_rows(v, v, table_ref, add=u)
    _pack(v, f_ref, n_lat)
    if mode == "qp":
        _zonal_rows(v, u, table_ref)
        _merid_rows(u, v, mir, index_ref, w_ref, depth)
        _pack(v, p_ref, n_lat)


def level_apply(mode, fields, table, index, merid_w, n_lat, padded):
    shape = fields[0].shape
    n_dev, per, rl, block = shape
    nb = n_dev // n_lat
    level_shape = (n_lat * rl, nb, padded, block)
    depth = merid_w.shape[0] - 1
    vmem = pl.BlockSpec(memory_space=pltpu.MemorySpace.VMEM)
    outs = 2 if mode == "qp" else 1
    result = pl.pallas_call(
        functools.partial(_kernel, mode, depth, n_lat),
        out_shape=[jax.ShapeDtypeStruct(shape, jnp.float32)] * outs,
        in_specs=[vmem] * (len(fields) + 2) + [pl.BlockSpec(memory_space=pltpu.MemorySpace.SMEM)],
        out_specs=[vmem] * outs,
        scratch_shapes=[
            pltpu.VMEM(level_shape, jnp.float32),
            pltpu.VMEM(level_shape, jnp.float32),
            pltpu.VMEM((2 * depth, nb, padded, block), jnp.float32),
        ],
        compiler_params=pltpu.CompilerParams(vmem_limit_bytes=60 * 1024 * 1024),
    )(*fields, table, index, merid_w)
    return result if outs == 2 else result[0]


def per_device(gradient, obs_weight, half_width, zonal_coef, mirror_map, merid_coef, vertical_map):
    n_lon = lax.axis_size("lon")
    n_lat = lax.axis_size("lat")
    n_dev = n_lon * n_lat
    lev, rows, cols = gradient.shape
    per = -(-lev // n_dev)
    padded = -(-per // 8) * 8 if per >= 4 else per
    width = zonal_coef.shape[1] - 1
    merid_w = merid_weights(merid_coef)

    def exchange(parts):
        return lax.all_to_all(parts, AXES, 0, 0, tiled=True)

    padded_lev = n_dev * per

    def col_parts(x):
        x = jnp.pad(x, ((0, padded_lev - x.shape[0]), (0, 0), (0, 0)))
        return x.reshape(n_dev, per, rows, cols)

    def to_column(z):
        return z.reshape(padded_lev, rows, cols)

    def to_output(z):
        return z.reshape(padded_lev, rows, cols)[:lev]

    vertical_pad = jnp.pad(vertical_map, ((0, 0), (0, padded_lev - lev)))

    lanes = cols if rows >= 4 else 1

    def slab(values):
        flat = jnp.repeat(values, lanes)
        flat = jnp.zeros((rows * cols,), jnp.float32).at[: flat.shape[0]].set(flat)
        return jnp.broadcast_to(flat.reshape(1, 1, rows, cols), (n_dev, 1, rows, cols))

    def totals(piece):
        flat = piece.reshape(n_dev, rows * cols)[:, : 4 * lanes].reshape(n_dev, 4, lanes)
        return jnp.sum(flat, axis=0)

    params = jnp.concatenate(
        [mirror_map.astype(jnp.float32), zonal_weights(half_width, zonal_coef).reshape(-1)]
    )
    slab_count = -(-params.shape[0] // (rows * cols))
    params = jnp.pad(params, (0, slab_count * rows * cols - params.shape[0]))
    params = params.reshape(1, slab_count, rows, cols)
    got = exchange(
        jnp.concatenate(
            [col_parts(gradient), jnp.broadcast_to(params, (n_dev, slab_count, rows, cols))], axis=1
        )
    )
    residual = got[:, :per]
    received = got[:, per:].reshape(n_lon, n_lat, slab_count * rows * cols)
    mirror_all = received[:, 0, :cols].reshape(n_lon * cols).astype(jnp.int32)
    zonal_all = received[0, :, cols : cols + rows * (width + 1)].reshape(n_lat * rows, width + 1)
    table = zonal_tables(zonal_all, cols)
    onehot = mirror_tables(mirror_all, cols)

    def forward(x):
        return level_apply("p", (x,), table, onehot, merid_w, n_lat, padded)

    def middle(y):
        lifted = jnp.einsum("kl,lji->kji", vertical_pad, y, precision=HI)
        return jnp.einsum("lk,lji->kji", vertical_pad, obs_weight * lifted, precision=HI)

    def image(x, px_col, mode):
        return level_apply(
            mode, (exchange(col_parts(middle(px_col))), x), table, onehot, merid_w, n_lat, padded
        )

    res_col = gradient
    inc_col = jnp.zeros_like(gradient)
    pres_col = to_column(exchange(forward(residual)))
    for outer in range(OUTER):
        last = outer == OUTER - 1
        first, pfirst = image(residual, pres_col, "qp")
        got = exchange(jnp.concatenate([pfirst, first], axis=1))
        pfirst_col = to_column(got[:, :per])
        first_col = to_output(got[:, per:])
        if last:
            second = image(first, pfirst_col, "q")
        else:
            second, psecond = image(first, pfirst_col, "qp")
        sums = jnp.stack(
            [
                jnp.sum(residual * residual),
                jnp.sum(residual * first),
                jnp.sum(first * first),
                jnp.sum(first * second),
            ]
        )
        parts = [(second)]
        if not last:
            parts.append((psecond))
        got = exchange(jnp.concatenate(parts + [slab(sums)], axis=1))
        second_col = to_output(got[:, :per])
        total = totals(got[:, len(parts) * per])
        sum_rr, sum_rf, sum_ff, sum_fs = total[0], total[1], total[2], total[3]
        determinant = sum_rf * sum_fs - sum_ff * sum_ff
        coef_one = (sum_fs * sum_rr - sum_ff * sum_rf) / determinant
        coef_two = (sum_rf * sum_rf - sum_ff * sum_rr) / determinant
        inc_col = inc_col + coef_one * res_col + coef_two * first_col
        res_col = res_col - coef_one * first_col - coef_two * second_col
        if not last:
            psecond_col = to_column(got[:, per : 2 * per])
            residual = residual - coef_one * first - coef_two * second
            pres_col = pres_col - coef_one * pfirst_col - coef_two * psecond_col
    return (inc_col, res_col)


def solution(mesh):
    placed = (
        P(None, "lat", "lon"),
        P(None, "lat", "lon"),
        P("lat"),
        P("lat", None),
        P("lon"),
        P(),
        P(),
    )
    return jax.shard_map(
        per_device,
        mesh=mesh,
        in_specs=placed,
        out_specs=(P(None, "lat", "lon"), P(None, "lat", "lon")),
        check_vma=False,
    )
```

```python
import functools

import jax
import jax.numpy as jnp
from jax import lax
from jax.experimental import pallas as pl
from jax.experimental.pallas import tpu as pltpu
from jax.sharding import PartitionSpec as P

OUTER = 2
AXES = ("lon", "lat")
HI = lax.Precision.HIGHEST
KERNEL_PRECISION = lax.Precision.HIGH


def zonal_weights(half_width, zonal_coef):
    tap_ids = jnp.arange(zonal_coef.shape[1], dtype=jnp.int32)
    kept = jnp.where(
        tap_ids[None, :] <= half_width[:, None], zonal_coef, jnp.zeros_like(zonal_coef)
    )
    scaling = jnp.sqrt(kept[:, 0] ** 2 + 2.0 * jnp.sum(kept[:, 1:] ** 2, axis=1))
    return kept / scaling[:, None]


def merid_weights(merid_coef):
    norm_value = jnp.sqrt(merid_coef[0] ** 2 + 2.0 * jnp.sum(merid_coef[1:] ** 2))
    return merid_coef / norm_value


def zonal_tables(weights, block):
    width = weights.shape[1] - 1
    positions = jnp.arange(3 * block, dtype=jnp.int32)
    columns = jnp.arange(block, dtype=jnp.int32)
    tap_ids = jnp.arange(width + 1, dtype=jnp.int32)
    distance = jnp.abs(positions[:, None] - block - columns[None, :])
    selector = (distance[:, :, None] == tap_ids[None, None, :]).astype(jnp.float32)
    table = jnp.einsum("pct,jt->jpc", selector, weights, precision=HI)
    table = table.reshape(weights.shape[0], 3, block, block)
    half = block // 2
    outer = jnp.concatenate([table[:, 2, :half], table[:, 0, half:]], axis=1)
    return jnp.stack([table[:, 1], outer], axis=1)


def mirror_tables(mirror_all, block):
    return (mirror_all % block).reshape(mirror_all.shape[0] // block, block)


def _dot(a, b):
    return jnp.dot(a, b, preferred_element_type=jnp.float32, precision=KERNEL_PRECISION)


def _zonal_rows(src, dst, table_ref, add=None):
    rows, nb, lp, block = src.shape
    lane = lax.broadcasted_iota(jnp.int32, (nb * lp, block), 1)
    for j in range(rows):
        mid = src[j]
        prev = jnp.concatenate([mid[nb - 1 :], mid[: nb - 1]], axis=0) if nb > 1 else mid
        nxt = jnp.concatenate([mid[1:], mid[:1]], axis=0) if nb > 1 else mid
        outer = jnp.where(
            lane >= block // 2, prev.reshape(nb * lp, block), nxt.reshape(nb * lp, block)
        )
        acc = _dot(mid.reshape(nb * lp, block), table_ref[j, 0]) + _dot(outer, table_ref[j, 1])
        acc = acc.reshape(nb, lp, block)
        if add is not None:
            acc = acc + add[j]
        dst[j] = acc


def _merid_rows(src, dst, mir, index_ref, w_ref, depth):
    rows, nb, lp, block = src.shape
    half = nb // 2

    def mirror_block(b, carry):
        sb = lax.rem(b + half, nb)
        polar = jnp.concatenate(
            [src[pl.ds(0, depth), pl.ds(sb, 1)], src[pl.ds(rows - depth, depth), pl.ds(sb, 1)]],
            axis=0,
        )
        source = lax.broadcasted_iota(jnp.int32, (block, block), 0)
        onehot = (source == index_ref[pl.ds(b, 1), :]).astype(jnp.float32)
        out = _dot(polar.reshape(2 * depth * lp, block), onehot)
        mir[:, pl.ds(b, 1)] = out.reshape(2 * depth, 1, lp, block)
        return carry

    lax.fori_loop(0, nb, mirror_block, 0)

    def row(k):
        if k < 0:
            return mir[-1 - k]
        if k >= rows:
            return mir[depth + (rows - 1 - (k - rows)) - (rows - depth)]
        return src[k]

    for j in range(rows):
        acc = w_ref[0] * src[j]
        for o in range(1, depth + 1):
            acc = acc + w_ref[o] * (row(j - o) + row(j + o))
        dst[j] = acc


def _unpack(parts_ref, off, dst, n_lat, per):
    rl = parts_ref.shape[2]
    nb = dst.shape[1]

    def one_block(b, carry):
        for a in range(n_lat):
            for lev in range(per):
                tile = parts_ref[b * n_lat + a, off + lev]
                for r in range(rl):
                    dst[a * rl + r, pl.ds(b, 1), pl.ds(lev, 1), :] = tile[r : r + 1].reshape(1, 1, -1)
        return carry

    lax.fori_loop(0, nb, one_block, 0)


def _pack(src, parts_ref, off, n_lat, per):
    rl = parts_ref.shape[2]
    nb = src.shape[1]

    def one_block(b, carry):
        for a in range(n_lat):
            for lev in range(per):
                tile = jnp.concatenate(
                    [src[a * rl + r, pl.ds(b, 1), pl.ds(lev, 1), :].reshape(1, -1) for r in range(rl)],
                    axis=0,
                )
                parts_ref[b * n_lat + a, off + lev] = tile
        return carry

    lax.fori_loop(0, nb, one_block, 0)


def _kernel(spec, *refs):
    depth, n_lat, per, x_off, r_off, offsets, has_a, has_r = spec
    refs = list(refs)
    a_ref = refs.pop(0) if has_a else None
    x_ref = refs.pop(0)
    r_ref = refs.pop(0) if has_r else None
    table_ref, index_ref, w_ref, out_ref, u, v, mir = refs
    if a_ref is None:
        _unpack(x_ref, x_off, u, n_lat, per)
        _zonal_rows(u, v, table_ref)
        _merid_rows(v, u, mir, index_ref, w_ref, depth)
        _pack(u, out_ref, offsets["p"], n_lat, per)
        return
    _unpack(a_ref, 0, u, n_lat, per)
    _merid_rows(u, v, mir, index_ref, w_ref, depth)
    _unpack(x_ref, x_off, u, n_lat, per)
    _zonal_rows(v, v, table_ref, add=u)
    _pack(v, out_ref, offsets["f"], n_lat, per)
    if "p" in offsets:
        _zonal_rows(v, u, table_ref)
        _merid_rows(u, v, mir, index_ref, w_ref, depth)
        _pack(v, out_ref, offsets["p"], n_lat, per)
    if "slab" in offsets:
        res = r_ref[:, pl.ds(r_off, per)]
        fst = x_ref[:, pl.ds(x_off, per)]
        snd = out_ref[:, pl.ds(offsets["f"], per)]
        sums = [jnp.sum(res * res), jnp.sum(res * fst), jnp.sum(fst * fst), jnp.sum(fst * snd)]
        n_dev, _, rl, block = out_ref.shape
        row = lax.broadcasted_iota(jnp.int32, (rl, block), 0)
        tile = jnp.zeros((rl, block), jnp.float32)
        for i, value in enumerate(sums):
            tile = jnp.where(row == i, value, tile)
        out_ref[:, offsets["slab"]] = jnp.broadcast_to(tile[None], (n_dev, rl, block))


def level_apply(sections, a, x, x_off, r, r_off, table, index, merid_w, n_lat, per, padded):
    n_dev, _, rl, block = x.shape
    nb = n_dev // n_lat
    level_shape = (n_lat * rl, nb, padded, block)
    depth = merid_w.shape[0] - 1
    offsets = {}
    levels = 0
    for name in sections:
        offsets[name] = levels
        levels += 1 if name == "slab" else per
    spec = (depth, n_lat, per, x_off, r_off, offsets, a is not None, r is not None)
    fields = [f for f in (a, x, r) if f is not None]
    vmem = pl.BlockSpec(memory_space=pltpu.MemorySpace.VMEM)
    return pl.pallas_call(
        functools.partial(_kernel, spec),
        out_shape=jax.ShapeDtypeStruct((n_dev, levels, rl, block), jnp.float32),
        in_specs=[vmem] * (len(fields) + 2) + [pl.BlockSpec(memory_space=pltpu.MemorySpace.SMEM)],
        out_specs=vmem,
        scratch_shapes=[
            pltpu.VMEM(level_shape, jnp.float32),
            pltpu.VMEM(level_shape, jnp.float32),
            pltpu.VMEM((2 * depth, nb, padded, block), jnp.float32),
        ],
        compiler_params=pltpu.CompilerParams(vmem_limit_bytes=60 * 1024 * 1024),
    )(*fields, table, index, merid_w)


def per_device(gradient, obs_weight, half_width, zonal_coef, mirror_map, merid_coef, vertical_map):
    n_lon = lax.axis_size("lon")
    n_lat = lax.axis_size("lat")
    n_dev = n_lon * n_lat
    lev, rows, cols = gradient.shape
    per = -(-lev // n_dev)
    padded = -(-per // 8) * 8 if per >= 4 else per
    width = zonal_coef.shape[1] - 1
    merid_w = merid_weights(merid_coef)

    def exchange(parts):
        return lax.all_to_all(parts, AXES, 0, 0, tiled=True)

    padded_lev = n_dev * per

    def col_parts(x):
        x = jnp.pad(x, ((0, padded_lev - x.shape[0]), (0, 0), (0, 0)))
        return x.reshape(n_dev, per, rows, cols)

    def to_column(z):
        return z.reshape(padded_lev, rows, cols)

    def to_output(z):
        return z.reshape(padded_lev, rows, cols)[:lev]

    vertical_pad = jnp.pad(vertical_map, ((0, 0), (0, padded_lev - lev)))

    lanes = cols if rows >= 4 else 1

    def slab(values):
        flat = jnp.repeat(values, lanes)
        flat = jnp.zeros((rows * cols,), jnp.float32).at[: flat.shape[0]].set(flat)
        return jnp.broadcast_to(flat.reshape(1, 1, rows, cols), (n_dev, 1, rows, cols))

    def levels_of(sections):
        return sum(1 if name == "slab" else per for name in sections)

    def totals(piece):
        flat = piece.reshape(n_dev, rows * cols)[:, : 4 * lanes].reshape(n_dev, 4, lanes)
        return jnp.sum(flat, axis=0)

    params = jnp.concatenate(
        [mirror_map.astype(jnp.float32), zonal_weights(half_width, zonal_coef).reshape(-1)]
    )
    slab_count = -(-params.shape[0] // (rows * cols))
    params = jnp.pad(params, (0, slab_count * rows * cols - params.shape[0]))
    params = params.reshape(1, slab_count, rows, cols)
    got = exchange(
        jnp.concatenate(
            [col_parts(gradient), jnp.broadcast_to(params, (n_dev, slab_count, rows, cols))], axis=1
        )
    )
    received = got[:, per:].reshape(n_lon, n_lat, slab_count * rows * cols)
    mirror_all = received[:, 0, :cols].reshape(n_lon * cols).astype(jnp.int32)
    zonal_all = received[0, :, cols : cols + rows * (width + 1)].reshape(n_lat * rows, width + 1)
    table = zonal_tables(zonal_all, cols)
    onehot = mirror_tables(mirror_all, cols)

    def apply(sections, a, x, x_off, r=None, r_off=0):
        return level_apply(
            sections, a, x, x_off, r, r_off, table, onehot, merid_w, n_lat, per, padded
        )

    def middle(y):
        lifted = jnp.einsum("kl,lji->kji", vertical_pad, y, precision=HI)
        return jnp.einsum("lk,lji->kji", vertical_pad, obs_weight * lifted, precision=HI)

    def lowered(px_col):
        return exchange(col_parts(middle(px_col)))

    res_col = gradient
    inc_col = jnp.zeros_like(gradient)
    res_buf = got
    pres_col = to_column(exchange(apply(("p",), None, res_buf, 0)))
    for outer in range(OUTER):
        last = outer == OUTER - 1
        first_buf = apply(("p", "f"), lowered(pres_col), res_buf, 0)
        got = exchange(first_buf)
        pfirst_col = to_column(got[:, :per])
        first_col = to_output(got[:, per:])
        sections = ("f", "slab") if last else ("f", "p", "slab")
        second_buf = apply(sections, lowered(pfirst_col), first_buf, per, res_buf, 0)
        got = exchange(second_buf)
        second_col = to_output(got[:, :per])
        total = totals(got[:, levels_of(sections) - 1])
        sum_rr, sum_rf, sum_ff, sum_fs = total[0], total[1], total[2], total[3]
        determinant = sum_rf * sum_fs - sum_ff * sum_ff
        coef_one = (sum_fs * sum_rr - sum_ff * sum_rf) / determinant
        coef_two = (sum_rf * sum_rf - sum_ff * sum_rr) / determinant
        inc_col = inc_col + coef_one * res_col + coef_two * first_col
        res_col = res_col - coef_one * first_col - coef_two * second_col
        if not last:
            psecond_col = to_column(got[:, per : 2 * per])
            res_buf = (
                res_buf[:, :per]
                - coef_one * first_buf[:, per : 2 * per]
                - coef_two * second_buf[:, :per]
            )
            pres_col = pres_col - coef_one * pfirst_col - coef_two * psecond_col
    return (inc_col, res_col)


def solution(mesh):
    placed = (
        P(None, "lat", "lon"),
        P(None, "lat", "lon"),
        P("lat"),
        P("lat", None),
        P("lon"),
        P(),
        P(),
    )
    return jax.shard_map(
        per_device,
        mesh=mesh,
        in_specs=placed,
        out_specs=(P(None, "lat", "lon"), P(None, "lat", "lon")),
        check_vma=False,
    )
```

```python
import functools

import jax
import jax.numpy as jnp
from jax import lax
from jax.experimental import pallas as pl
from jax.experimental.pallas import tpu as pltpu
from jax.sharding import PartitionSpec as P

OUTER = 2
AXES = ("lon", "lat")
HI = lax.Precision.HIGHEST
KERNEL_PRECISION = lax.Precision.HIGH


def zonal_weights(half_width, zonal_coef):
    tap_ids = jnp.arange(zonal_coef.shape[1], dtype=jnp.int32)
    kept = jnp.where(
        tap_ids[None, :] <= half_width[:, None], zonal_coef, jnp.zeros_like(zonal_coef)
    )
    scaling = jnp.sqrt(kept[:, 0] ** 2 + 2.0 * jnp.sum(kept[:, 1:] ** 2, axis=1))
    return kept / scaling[:, None]


def merid_weights(merid_coef):
    norm_value = jnp.sqrt(merid_coef[0] ** 2 + 2.0 * jnp.sum(merid_coef[1:] ** 2))
    return merid_coef / norm_value


def zonal_tables(weights, block):
    width = weights.shape[1] - 1
    positions = jnp.arange(3 * block, dtype=jnp.int32)
    columns = jnp.arange(block, dtype=jnp.int32)
    tap_ids = jnp.arange(width + 1, dtype=jnp.int32)
    distance = jnp.abs(positions[:, None] - block - columns[None, :])
    selector = (distance[:, :, None] == tap_ids[None, None, :]).astype(jnp.float32)
    table = jnp.einsum("pct,jt->jpc", selector, weights, precision=HI)
    table = table.reshape(weights.shape[0], 3, block, block)
    half = block // 2
    outer = jnp.concatenate([table[:, 2, :half], table[:, 0, half:]], axis=1)
    return jnp.concatenate([table[:, 1], outer], axis=1)


def mirror_tables(mirror_all, block):
    return (mirror_all % block).reshape(mirror_all.shape[0] // block, block)


def _dot(a, b):
    return jnp.dot(a, b, preferred_element_type=jnp.float32, precision=KERNEL_PRECISION)


def _zonal_rows(src, dst, table_ref, add=None):
    rows, nb, lp, block = src.shape
    lane = lax.broadcasted_iota(jnp.int32, (nb * lp, block), 1)
    for j in range(rows):
        mid = src[j]
        prev = jnp.concatenate([mid[nb - 1 :], mid[: nb - 1]], axis=0) if nb > 1 else mid
        nxt = jnp.concatenate([mid[1:], mid[:1]], axis=0) if nb > 1 else mid
        outer = jnp.where(
            lane >= block // 2, prev.reshape(nb * lp, block), nxt.reshape(nb * lp, block)
        )
        acc = _dot(jnp.concatenate([mid.reshape(nb * lp, block), outer], axis=1), table_ref[j])
        acc = acc.reshape(nb, lp, block)
        if add is not None:
            acc = acc + add[j]
        dst[j] = acc


def _merid_rows(src, dst, mir, index_ref, w_ref, depth):
    rows, nb, lp, block = src.shape
    half = nb // 2

    def mirror_block(b, carry):
        sb = lax.rem(b + half, nb)
        polar = jnp.concatenate(
            [src[pl.ds(0, depth), pl.ds(sb, 1)], src[pl.ds(rows - depth, depth), pl.ds(sb, 1)]],
            axis=0,
        )
        source = lax.broadcasted_iota(jnp.int32, (block, block), 0)
        onehot = (source == index_ref[pl.ds(b, 1), :]).astype(jnp.bfloat16)
        polar = polar.reshape(2 * depth * lp, block)
        high = polar.astype(jnp.bfloat16)
        low = (polar - high.astype(jnp.float32)).astype(jnp.bfloat16)
        out = jnp.dot(high, onehot, preferred_element_type=jnp.float32) + jnp.dot(
            low, onehot, preferred_element_type=jnp.float32
        )
        mir[:, pl.ds(b, 1)] = out.reshape(2 * depth, 1, lp, block)
        return carry

    lax.fori_loop(0, nb, mirror_block, 0)

    def row(k):
        if k < 0:
            return mir[-1 - k]
        if k >= rows:
            return mir[depth + (rows - 1 - (k - rows)) - (rows - depth)]
        return src[k]

    for j in range(rows):
        acc = w_ref[0] * src[j]
        for o in range(1, depth + 1):
            acc = acc + w_ref[o] * (row(j - o) + row(j + o))
        dst[j] = acc


def _unpack(parts_ref, off, dst, n_lat, per):
    rl = parts_ref.shape[2]
    nb = dst.shape[1]

    def one_block(b, carry):
        for a in range(n_lat):
            for lev in range(per):
                tile = parts_ref[b * n_lat + a, off + lev]
                for r in range(rl):
                    dst[a * rl + r, pl.ds(b, 1), pl.ds(lev, 1), :] = tile[r : r + 1].reshape(1, 1, -1)
        return carry

    lax.fori_loop(0, nb, one_block, 0)


def _pack(src, parts_ref, off, n_lat, per):
    rl = parts_ref.shape[2]
    nb = src.shape[1]

    def one_block(b, carry):
        for a in range(n_lat):
            for lev in range(per):
                tile = jnp.concatenate(
                    [src[a * rl + r, pl.ds(b, 1), pl.ds(lev, 1), :].reshape(1, -1) for r in range(rl)],
                    axis=0,
                )
                parts_ref[b * n_lat + a, off + lev] = tile
        return carry

    lax.fori_loop(0, nb, one_block, 0)


def _kernel(spec, *refs):
    depth, n_lat, per, x_off, r_off, offsets, has_a, has_r = spec
    refs = list(refs)
    a_ref = refs.pop(0) if has_a else None
    x_ref = refs.pop(0)
    r_ref = refs.pop(0) if has_r else None
    table_ref, index_ref, w_ref, out_ref, u, v, mir = refs
    if a_ref is None:
        _unpack(x_ref, x_off, u, n_lat, per)
        _zonal_rows(u, v, table_ref)
        _merid_rows(v, u, mir, index_ref, w_ref, depth)
        _pack(u, out_ref, offsets["p"], n_lat, per)
        return
    _unpack(a_ref, 0, u, n_lat, per)
    _merid_rows(u, v, mir, index_ref, w_ref, depth)
    _unpack(x_ref, x_off, u, n_lat, per)
    _zonal_rows(v, v, table_ref, add=u)
    _pack(v, out_ref, offsets["f"], n_lat, per)
    if "p" in offsets:
        _zonal_rows(v, u, table_ref)
        _merid_rows(u, v, mir, index_ref, w_ref, depth)
        _pack(v, out_ref, offsets["p"], n_lat, per)
    if "slab" in offsets:
        res = r_ref[:, pl.ds(r_off, per)]
        fst = x_ref[:, pl.ds(x_off, per)]
        snd = out_ref[:, pl.ds(offsets["f"], per)]
        sums = [jnp.sum(res * res), jnp.sum(res * fst), jnp.sum(fst * fst), jnp.sum(fst * snd)]
        n_dev, _, rl, block = out_ref.shape
        row = lax.broadcasted_iota(jnp.int32, (rl, block), 0)
        tile = jnp.zeros((rl, block), jnp.float32)
        for i, value in enumerate(sums):
            tile = jnp.where(row == i, value, tile)
        out_ref[:, offsets["slab"]] = jnp.broadcast_to(tile[None], (n_dev, rl, block))


def level_apply(sections, a, x, x_off, r, r_off, table, index, merid_w, n_lat, per, padded):
    n_dev, _, rl, block = x.shape
    nb = n_dev // n_lat
    level_shape = (n_lat * rl, nb, padded, block)
    depth = merid_w.shape[0] - 1
    offsets = {}
    levels = 0
    for name in sections:
        offsets[name] = levels
        levels += 1 if name == "slab" else per
    spec = (depth, n_lat, per, x_off, r_off, offsets, a is not None, r is not None)
    fields = [f for f in (a, x, r) if f is not None]
    vmem = pl.BlockSpec(memory_space=pltpu.MemorySpace.VMEM)
    return pl.pallas_call(
        functools.partial(_kernel, spec),
        out_shape=jax.ShapeDtypeStruct((n_dev, levels, rl, block), jnp.float32),
        in_specs=[vmem] * (len(fields) + 2) + [pl.BlockSpec(memory_space=pltpu.MemorySpace.SMEM)],
        out_specs=vmem,
        scratch_shapes=[
            pltpu.VMEM(level_shape, jnp.float32),
            pltpu.VMEM(level_shape, jnp.float32),
            pltpu.VMEM((2 * depth, nb, padded, block), jnp.float32),
        ],
        compiler_params=pltpu.CompilerParams(vmem_limit_bytes=60 * 1024 * 1024),
    )(*fields, table, index, merid_w)


def per_device(gradient, obs_weight, half_width, zonal_coef, mirror_map, merid_coef, vertical_map):
    n_lon = lax.axis_size("lon")
    n_lat = lax.axis_size("lat")
    n_dev = n_lon * n_lat
    lev, rows, cols = gradient.shape
    per = -(-lev // n_dev)
    padded = -(-per // 8) * 8 if per >= 4 else per
    width = zonal_coef.shape[1] - 1
    merid_w = merid_weights(merid_coef)

    def exchange(parts):
        return lax.all_to_all(parts, AXES, 0, 0, tiled=True)

    padded_lev = n_dev * per

    def col_parts(x):
        x = jnp.pad(x, ((0, padded_lev - x.shape[0]), (0, 0), (0, 0)))
        return x.reshape(n_dev, per, rows, cols)

    def to_column(z):
        return z.reshape(padded_lev, rows, cols)

    def to_output(z):
        return z.reshape(padded_lev, rows, cols)[:lev]

    vertical_pad = jnp.pad(vertical_map, ((0, 0), (0, padded_lev - lev)))

    lanes = cols if rows >= 4 else 1

    def slab(values):
        flat = jnp.repeat(values, lanes)
        flat = jnp.zeros((rows * cols,), jnp.float32).at[: flat.shape[0]].set(flat)
        return jnp.broadcast_to(flat.reshape(1, 1, rows, cols), (n_dev, 1, rows, cols))

    def levels_of(sections):
        return sum(1 if name == "slab" else per for name in sections)

    def totals(piece):
        flat = piece.reshape(n_dev, rows * cols)[:, : 4 * lanes].reshape(n_dev, 4, lanes)
        return jnp.sum(flat, axis=0)

    params = jnp.concatenate(
        [mirror_map.astype(jnp.float32), zonal_weights(half_width, zonal_coef).reshape(-1)]
    )
    slab_count = -(-params.shape[0] // (rows * cols))
    params = jnp.pad(params, (0, slab_count * rows * cols - params.shape[0]))
    params = params.reshape(1, slab_count, rows, cols)
    got = exchange(
        jnp.concatenate(
            [col_parts(gradient), jnp.broadcast_to(params, (n_dev, slab_count, rows, cols))], axis=1
        )
    )
    received = got[:, per:].reshape(n_lon, n_lat, slab_count * rows * cols)
    mirror_all = received[:, 0, :cols].reshape(n_lon * cols).astype(jnp.int32)
    zonal_all = received[0, :, cols : cols + rows * (width + 1)].reshape(n_lat * rows, width + 1)
    table = zonal_tables(zonal_all, cols)
    onehot = mirror_tables(mirror_all, cols)

    def apply(sections, a, x, x_off, r=None, r_off=0):
        return level_apply(
            sections, a, x, x_off, r, r_off, table, onehot, merid_w, n_lat, per, padded
        )

    def middle(y):
        lifted = jnp.einsum("kl,lji->kji", vertical_pad, y, precision=HI)
        return jnp.einsum("lk,lji->kji", vertical_pad, obs_weight * lifted, precision=HI)

    def lowered(px_col):
        return exchange(col_parts(middle(px_col)))

    res_col = gradient
    inc_col = jnp.zeros_like(gradient)
    res_buf = got
    pres_col = to_column(exchange(apply(("p",), None, res_buf, 0)))
    for outer in range(OUTER):
        last = outer == OUTER - 1
        first_buf = apply(("p", "f"), lowered(pres_col), res_buf, 0)
        got = exchange(first_buf)
        pfirst_col = to_column(got[:, :per])
        first_col = to_output(got[:, per:])
        sections = ("f", "slab") if last else ("f", "p", "slab")
        second_buf = apply(sections, lowered(pfirst_col), first_buf, per, res_buf, 0)
        got = exchange(second_buf)
        second_col = to_output(got[:, :per])
        total = totals(got[:, levels_of(sections) - 1])
        sum_rr, sum_rf, sum_ff, sum_fs = total[0], total[1], total[2], total[3]
        determinant = sum_rf * sum_fs - sum_ff * sum_ff
        coef_one = (sum_fs * sum_rr - sum_ff * sum_rf) / determinant
        coef_two = (sum_rf * sum_rf - sum_ff * sum_rr) / determinant
        inc_col = inc_col + coef_one * res_col + coef_two * first_col
        res_col = res_col - coef_one * first_col - coef_two * second_col
        if not last:
            psecond_col = to_column(got[:, per : 2 * per])
            res_buf = (
                res_buf[:, :per]
                - coef_one * first_buf[:, per : 2 * per]
                - coef_two * second_buf[:, :per]
            )
            pres_col = pres_col - coef_one * pfirst_col - coef_two * psecond_col
    return (inc_col, res_col)


def solution(mesh):
    placed = (
        P(None, "lat", "lon"),
        P(None, "lat", "lon"),
        P("lat"),
        P("lat", None),
        P("lon"),
        P(),
        P(),
    )
    return jax.shard_map(
        per_device,
        mesh=mesh,
        in_specs=placed,
        out_specs=(P(None, "lat", "lon"), P(None, "lat", "lon")),
        check_vma=False,
    )
```

```python
import functools

import jax
import jax.numpy as jnp
from jax import lax
from jax.experimental import pallas as pl
from jax.experimental.pallas import tpu as pltpu
from jax.sharding import PartitionSpec as P

OUTER = 2
AXES = ("lon", "lat")
HI = lax.Precision.HIGHEST
KERNEL_PRECISION = lax.Precision.HIGH


def zonal_weights(half_width, zonal_coef):
    tap_ids = jnp.arange(zonal_coef.shape[1], dtype=jnp.int32)
    kept = jnp.where(
        tap_ids[None, :] <= half_width[:, None], zonal_coef, jnp.zeros_like(zonal_coef)
    )
    scaling = jnp.sqrt(kept[:, 0] ** 2 + 2.0 * jnp.sum(kept[:, 1:] ** 2, axis=1))
    return kept / scaling[:, None]


def merid_weights(merid_coef):
    norm_value = jnp.sqrt(merid_coef[0] ** 2 + 2.0 * jnp.sum(merid_coef[1:] ** 2))
    return merid_coef / norm_value


def zonal_tables(weights, block):
    width = weights.shape[1] - 1
    positions = jnp.arange(3 * block, dtype=jnp.int32)
    columns = jnp.arange(block, dtype=jnp.int32)
    tap_ids = jnp.arange(width + 1, dtype=jnp.int32)
    distance = jnp.abs(positions[:, None] - block - columns[None, :])
    selector = (distance[:, :, None] == tap_ids[None, None, :]).astype(jnp.float32)
    table = jnp.einsum("pct,jt->jpc", selector, weights, precision=HI)
    table = table.reshape(weights.shape[0], 3, block, block)
    half = block // 2
    outer = jnp.concatenate([table[:, 2, :half], table[:, 0, half:]], axis=1)
    return jnp.concatenate([table[:, 1], outer], axis=1)


def mirror_tables(mirror_all, block):
    return (mirror_all % block).reshape(mirror_all.shape[0] // block, block)


def _dot(a, b):
    return jnp.dot(a, b, preferred_element_type=jnp.float32, precision=KERNEL_PRECISION)


def _zonal_rows(src, dst, table_ref, add=None):
    rows, nb, lp, block = src.shape
    lane = lax.broadcasted_iota(jnp.int32, (nb * lp, block), 1)
    for j in range(rows):
        mid = src[j]
        prev = jnp.concatenate([mid[nb - 1 :], mid[: nb - 1]], axis=0) if nb > 1 else mid
        nxt = jnp.concatenate([mid[1:], mid[:1]], axis=0) if nb > 1 else mid
        outer = jnp.where(
            lane >= block // 2, prev.reshape(nb * lp, block), nxt.reshape(nb * lp, block)
        )
        acc = _dot(jnp.concatenate([mid.reshape(nb * lp, block), outer], axis=1), table_ref[j])
        acc = acc.reshape(nb, lp, block)
        if add is not None:
            acc = acc + add[j]
        dst[j] = acc


def _merid_rows(src, dst, mir, index_ref, w_ref, depth):
    rows, nb, lp, block = src.shape
    half = nb // 2

    def mirror_block(b, carry):
        sb = lax.rem(b + half, nb)
        polar = jnp.concatenate(
            [src[pl.ds(0, depth), pl.ds(sb, 1)], src[pl.ds(rows - depth, depth), pl.ds(sb, 1)]],
            axis=0,
        )
        source = lax.broadcasted_iota(jnp.int32, (block, block), 0)
        onehot = (source == index_ref[pl.ds(b, 1), :]).astype(jnp.bfloat16)
        polar = polar.reshape(2 * depth * lp, block)
        high = polar.astype(jnp.bfloat16)
        low = (polar - high.astype(jnp.float32)).astype(jnp.bfloat16)
        out = jnp.dot(high, onehot, preferred_element_type=jnp.float32) + jnp.dot(
            low, onehot, preferred_element_type=jnp.float32
        )
        mir[:, pl.ds(b, 1)] = out.reshape(2 * depth, 1, lp, block)
        return carry

    lax.fori_loop(0, nb, mirror_block, 0, unroll=nb <= 16)

    def row(k):
        if k < 0:
            return mir[-1 - k]
        if k >= rows:
            return mir[depth + (rows - 1 - (k - rows)) - (rows - depth)]
        return src[k]

    for j in range(rows):
        acc = w_ref[0] * src[j]
        for o in range(1, depth + 1):
            acc = acc + w_ref[o] * (row(j - o) + row(j + o))
        dst[j] = acc


def _unpack(parts_ref, off, dst, n_lat, per):
    rl = parts_ref.shape[2]
    nb = dst.shape[1]

    def one_block(b, carry):
        for a in range(n_lat):
            for lev in range(per):
                tile = parts_ref[b * n_lat + a, off + lev]
                for r in range(rl):
                    dst[a * rl + r, pl.ds(b, 1), pl.ds(lev, 1), :] = tile[r : r + 1].reshape(1, 1, -1)
        return carry

    lax.fori_loop(0, nb, one_block, 0, unroll=nb <= 16)


def _pack(src, parts_ref, off, n_lat, per):
    rl = parts_ref.shape[2]
    nb = src.shape[1]

    def one_block(b, carry):
        for a in range(n_lat):
            for lev in range(per):
                tile = jnp.concatenate(
                    [src[a * rl + r, pl.ds(b, 1), pl.ds(lev, 1), :].reshape(1, -1) for r in range(rl)],
                    axis=0,
                )
                parts_ref[b * n_lat + a, off + lev] = tile
        return carry

    lax.fori_loop(0, nb, one_block, 0, unroll=nb <= 16)


def _kernel(spec, *refs):
    depth, n_lat, per, x_off, r_off, offsets, has_a, has_r = spec
    refs = list(refs)
    a_ref = refs.pop(0) if has_a else None
    x_ref = refs.pop(0)
    r_ref = refs.pop(0) if has_r else None
    table_ref, index_ref, w_ref, out_ref, u, v, mir = refs
    if a_ref is None:
        _unpack(x_ref, x_off, u, n_lat, per)
        _zonal_rows(u, v, table_ref)
        _merid_rows(v, u, mir, index_ref, w_ref, depth)
        _pack(u, out_ref, offsets["p"], n_lat, per)
        return
    _unpack(a_ref, 0, u, n_lat, per)
    _merid_rows(u, v, mir, index_ref, w_ref, depth)
    _unpack(x_ref, x_off, u, n_lat, per)
    _zonal_rows(v, v, table_ref, add=u)
    _pack(v, out_ref, offsets["f"], n_lat, per)
    if "p" in offsets:
        _zonal_rows(v, u, table_ref)
        _merid_rows(u, v, mir, index_ref, w_ref, depth)
        _pack(v, out_ref, offsets["p"], n_lat, per)
    if "slab" in offsets:
        res = r_ref[:, pl.ds(r_off, per)]
        fst = x_ref[:, pl.ds(x_off, per)]
        snd = out_ref[:, pl.ds(offsets["f"], per)]
        sums = [jnp.sum(res * res), jnp.sum(res * fst), jnp.sum(fst * fst), jnp.sum(fst * snd)]
        n_dev, _, rl, block = out_ref.shape
        row = lax.broadcasted_iota(jnp.int32, (rl, block), 0)
        tile = jnp.zeros((rl, block), jnp.float32)
        for i, value in enumerate(sums):
            tile = jnp.where(row == i, value, tile)
        out_ref[:, offsets["slab"]] = jnp.broadcast_to(tile[None], (n_dev, rl, block))


def level_apply(sections, a, x, x_off, r, r_off, table, index, merid_w, n_lat, per, padded):
    n_dev, _, rl, block = x.shape
    nb = n_dev // n_lat
    level_shape = (n_lat * rl, nb, padded, block)
    depth = merid_w.shape[0] - 1
    offsets = {}
    levels = 0
    for name in sections:
        offsets[name] = levels
        levels += 1 if name == "slab" else per
    spec = (depth, n_lat, per, x_off, r_off, offsets, a is not None, r is not None)
    fields = [f for f in (a, x, r) if f is not None]
    vmem = pl.BlockSpec(memory_space=pltpu.MemorySpace.VMEM)
    return pl.pallas_call(
        functools.partial(_kernel, spec),
        out_shape=jax.ShapeDtypeStruct((n_dev, levels, rl, block), jnp.float32),
        in_specs=[vmem] * (len(fields) + 2) + [pl.BlockSpec(memory_space=pltpu.MemorySpace.SMEM)],
        out_specs=vmem,
        scratch_shapes=[
            pltpu.VMEM(level_shape, jnp.float32),
            pltpu.VMEM(level_shape, jnp.float32),
            pltpu.VMEM((2 * depth, nb, padded, block), jnp.float32),
        ],
        compiler_params=pltpu.CompilerParams(vmem_limit_bytes=60 * 1024 * 1024),
    )(*fields, table, index, merid_w)


def per_device(gradient, obs_weight, half_width, zonal_coef, mirror_map, merid_coef, vertical_map):
    n_lon = lax.axis_size("lon")
    n_lat = lax.axis_size("lat")
    n_dev = n_lon * n_lat
    lev, rows, cols = gradient.shape
    per = -(-lev // n_dev)
    padded = -(-per // 8) * 8 if per >= 4 else per
    width = zonal_coef.shape[1] - 1
    merid_w = merid_weights(merid_coef)

    def exchange(parts):
        return lax.all_to_all(parts, AXES, 0, 0, tiled=True)

    padded_lev = n_dev * per

    def col_parts(x):
        x = jnp.pad(x, ((0, padded_lev - x.shape[0]), (0, 0), (0, 0)))
        return x.reshape(n_dev, per, rows, cols)

    def to_column(z):
        return z.reshape(padded_lev, rows, cols)

    def to_output(z):
        return z.reshape(padded_lev, rows, cols)[:lev]

    vertical_pad = jnp.pad(vertical_map, ((0, 0), (0, padded_lev - lev)))

    lanes = cols if rows >= 4 else 1

    def slab(values):
        flat = jnp.repeat(values, lanes)
        flat = jnp.zeros((rows * cols,), jnp.float32).at[: flat.shape[0]].set(flat)
        return jnp.broadcast_to(flat.reshape(1, 1, rows, cols), (n_dev, 1, rows, cols))

    def levels_of(sections):
        return sum(1 if name == "slab" else per for name in sections)

    def totals(piece):
        flat = piece.reshape(n_dev, rows * cols)[:, : 4 * lanes].reshape(n_dev, 4, lanes)
        return jnp.sum(flat, axis=0)

    params = jnp.concatenate(
        [mirror_map.astype(jnp.float32), zonal_weights(half_width, zonal_coef).reshape(-1)]
    )
    slab_count = -(-params.shape[0] // (rows * cols))
    params = jnp.pad(params, (0, slab_count * rows * cols - params.shape[0]))
    params = params.reshape(1, slab_count, rows, cols)
    got = exchange(
        jnp.concatenate(
            [col_parts(gradient), jnp.broadcast_to(params, (n_dev, slab_count, rows, cols))], axis=1
        )
    )
    received = got[:, per:].reshape(n_lon, n_lat, slab_count * rows * cols)
    mirror_all = received[:, 0, :cols].reshape(n_lon * cols).astype(jnp.int32)
    zonal_all = received[0, :, cols : cols + rows * (width + 1)].reshape(n_lat * rows, width + 1)
    table = zonal_tables(zonal_all, cols)
    onehot = mirror_tables(mirror_all, cols)

    def apply(sections, a, x, x_off, r=None, r_off=0):
        return level_apply(
            sections, a, x, x_off, r, r_off, table, onehot, merid_w, n_lat, per, padded
        )

    def middle(y):
        lifted = jnp.einsum("kl,lji->kji", vertical_pad, y, precision=HI)
        return jnp.einsum("lk,lji->kji", vertical_pad, obs_weight * lifted, precision=HI)

    def lowered(px_col):
        return exchange(col_parts(middle(px_col)))

    res_col = gradient
    inc_col = jnp.zeros_like(gradient)
    res_buf = got
    pres_col = to_column(exchange(apply(("p",), None, res_buf, 0)))
    for outer in range(OUTER):
        last = outer == OUTER - 1
        first_buf = apply(("p", "f"), lowered(pres_col), res_buf, 0)
        got = exchange(first_buf)
        pfirst_col = to_column(got[:, :per])
        first_col = to_output(got[:, per:])
        sections = ("f", "slab") if last else ("f", "p", "slab")
        second_buf = apply(sections, lowered(pfirst_col), first_buf, per, res_buf, 0)
        got = exchange(second_buf)
        second_col = to_output(got[:, :per])
        total = totals(got[:, levels_of(sections) - 1])
        sum_rr, sum_rf, sum_ff, sum_fs = total[0], total[1], total[2], total[3]
        determinant = sum_rf * sum_fs - sum_ff * sum_ff
        coef_one = (sum_fs * sum_rr - sum_ff * sum_rf) / determinant
        coef_two = (sum_rf * sum_rf - sum_ff * sum_rr) / determinant
        inc_col = inc_col + coef_one * res_col + coef_two * first_col
        res_col = res_col - coef_one * first_col - coef_two * second_col
        if not last:
            psecond_col = to_column(got[:, per : 2 * per])
            res_buf = (
                res_buf[:, :per]
                - coef_one * first_buf[:, per : 2 * per]
                - coef_two * second_buf[:, :per]
            )
            pres_col = pres_col - coef_one * pfirst_col - coef_two * psecond_col
    return (inc_col, res_col)


def solution(mesh):
    placed = (
        P(None, "lat", "lon"),
        P(None, "lat", "lon"),
        P("lat"),
        P("lat", None),
        P("lon"),
        P(),
        P(),
    )
    return jax.shard_map(
        per_device,
        mesh=mesh,
        in_specs=placed,
        out_specs=(P(None, "lat", "lon"), P(None, "lat", "lon")),
        check_vma=False,
    )
```

```python
import functools

import jax
import jax.numpy as jnp
from jax import lax
from jax.experimental import pallas as pl
from jax.experimental.pallas import tpu as pltpu
from jax.sharding import PartitionSpec as P

OUTER = 2
AXES = ("lon", "lat")
HI = lax.Precision.HIGHEST
KERNEL_PRECISION = lax.Precision.HIGH


def zonal_weights(half_width, zonal_coef):
    tap_ids = jnp.arange(zonal_coef.shape[1], dtype=jnp.int32)
    kept = jnp.where(
        tap_ids[None, :] <= half_width[:, None], zonal_coef, jnp.zeros_like(zonal_coef)
    )
    scaling = jnp.sqrt(kept[:, 0] ** 2 + 2.0 * jnp.sum(kept[:, 1:] ** 2, axis=1))
    return kept / scaling[:, None]


def merid_weights(merid_coef):
    norm_value = jnp.sqrt(merid_coef[0] ** 2 + 2.0 * jnp.sum(merid_coef[1:] ** 2))
    return merid_coef / norm_value


def zonal_tables(weights, block):
    width = weights.shape[1] - 1
    source = jnp.arange(2 * block, dtype=jnp.int32)
    lane = source % block
    shift = jnp.where(source < block, 0, jnp.where(lane < block // 2, block, -block))
    columns = jnp.arange(block, dtype=jnp.int32)
    tap_ids = jnp.arange(width + 1, dtype=jnp.int32)
    distance = jnp.abs((lane + shift)[:, None] - columns[None, :])
    selector = (distance[:, :, None] == tap_ids[None, None, :]).astype(jnp.float32)
    return jnp.einsum("pct,jt->jpc", selector, weights, precision=HI)


def mirror_tables(mirror_all, block):
    return (mirror_all % block).reshape(mirror_all.shape[0] // block, block)


def _dot(a, b):
    return jnp.dot(a, b, preferred_element_type=jnp.float32, precision=KERNEL_PRECISION)


def _zonal_rows(src, dst, table_ref, add=None):
    rows, nb, lp, block = src.shape
    lane = lax.broadcasted_iota(jnp.int32, (nb * lp, block), 1)
    for j in range(rows):
        mid = src[j]
        prev = jnp.concatenate([mid[nb - 1 :], mid[: nb - 1]], axis=0) if nb > 1 else mid
        nxt = jnp.concatenate([mid[1:], mid[:1]], axis=0) if nb > 1 else mid
        outer = jnp.where(
            lane >= block // 2, prev.reshape(nb * lp, block), nxt.reshape(nb * lp, block)
        )
        acc = _dot(jnp.concatenate([mid.reshape(nb * lp, block), outer], axis=1), table_ref[j])
        acc = acc.reshape(nb, lp, block)
        if add is not None:
            acc = acc + add[j]
        dst[j] = acc


def _merid_rows(src, dst, mir, index_ref, w_ref, depth):
    rows, nb, lp, block = src.shape
    half = nb // 2

    def mirror_block(b, carry):
        sb = lax.rem(b + half, nb)
        polar = jnp.concatenate(
            [src[pl.ds(0, depth), pl.ds(sb, 1)], src[pl.ds(rows - depth, depth), pl.ds(sb, 1)]],
            axis=0,
        )
        source = lax.broadcasted_iota(jnp.int32, (block, block), 0)
        onehot = (source == index_ref[pl.ds(b, 1), :]).astype(jnp.bfloat16)
        polar = polar.reshape(2 * depth * lp, block)
        high = polar.astype(jnp.bfloat16)
        low = (polar - high.astype(jnp.float32)).astype(jnp.bfloat16)
        out = jnp.dot(high, onehot, preferred_element_type=jnp.float32) + jnp.dot(
            low, onehot, preferred_element_type=jnp.float32
        )
        mir[:, pl.ds(b, 1)] = out.reshape(2 * depth, 1, lp, block)
        return carry

    lax.fori_loop(0, nb, mirror_block, 0, unroll=nb <= 16)

    def row(k):
        if k < 0:
            return mir[-1 - k]
        if k >= rows:
            return mir[depth + (rows - 1 - (k - rows)) - (rows - depth)]
        return src[k]

    for j in range(rows):
        acc = w_ref[0] * src[j]
        for o in range(1, depth + 1):
            acc = acc + w_ref[o] * (row(j - o) + row(j + o))
        dst[j] = acc


def _unpack(parts_ref, off, dst, n_lat, per):
    rl = parts_ref.shape[2]
    nb = dst.shape[1]

    def one_block(b, carry):
        for a in range(n_lat):
            for lev in range(per):
                tile = parts_ref[b * n_lat + a, off + lev]
                for r in range(rl):
                    dst[a * rl + r, pl.ds(b, 1), pl.ds(lev, 1), :] = tile[r : r + 1].reshape(1, 1, -1)
        return carry

    lax.fori_loop(0, nb, one_block, 0, unroll=nb <= 16)


def _pack(src, parts_ref, off, n_lat, per):
    rl = parts_ref.shape[2]
    nb = src.shape[1]

    def one_block(b, carry):
        for a in range(n_lat):
            for lev in range(per):
                tile = jnp.concatenate(
                    [src[a * rl + r, pl.ds(b, 1), pl.ds(lev, 1), :].reshape(1, -1) for r in range(rl)],
                    axis=0,
                )
                parts_ref[b * n_lat + a, off + lev] = tile
        return carry

    lax.fori_loop(0, nb, one_block, 0, unroll=nb <= 16)


def _kernel(spec, *refs):
    depth, n_lat, per, x_off, r_off, offsets, has_a, has_r = spec
    refs = list(refs)
    a_ref = refs.pop(0) if has_a else None
    x_ref = refs.pop(0)
    r_ref = refs.pop(0) if has_r else None
    table_ref, index_ref, w_ref, out_ref, u, v, mir = refs
    if a_ref is None:
        _unpack(x_ref, x_off, u, n_lat, per)
        _zonal_rows(u, v, table_ref)
        _merid_rows(v, u, mir, index_ref, w_ref, depth)
        _pack(u, out_ref, offsets["p"], n_lat, per)
        return
    _unpack(a_ref, 0, u, n_lat, per)
    _merid_rows(u, v, mir, index_ref, w_ref, depth)
    _unpack(x_ref, x_off, u, n_lat, per)
    _zonal_rows(v, v, table_ref, add=u)
    _pack(v, out_ref, offsets["f"], n_lat, per)
    if "p" in offsets:
        _zonal_rows(v, u, table_ref)
        _merid_rows(u, v, mir, index_ref, w_ref, depth)
        _pack(v, out_ref, offsets["p"], n_lat, per)
    if "slab" in offsets:
        res = r_ref[:, pl.ds(r_off, per)]
        fst = x_ref[:, pl.ds(x_off, per)]
        snd = out_ref[:, pl.ds(offsets["f"], per)]
        sums = [jnp.sum(res * res), jnp.sum(res * fst), jnp.sum(fst * fst), jnp.sum(fst * snd)]
        n_dev, _, rl, block = out_ref.shape
        row = lax.broadcasted_iota(jnp.int32, (rl, block), 0)
        tile = jnp.zeros((rl, block), jnp.float32)
        for i, value in enumerate(sums):
            tile = jnp.where(row == i, value, tile)
        out_ref[:, offsets["slab"]] = jnp.broadcast_to(tile[None], (n_dev, rl, block))


def level_apply(sections, a, x, x_off, r, r_off, table, index, merid_w, n_lat, per, padded):
    n_dev, _, rl, block = x.shape
    nb = n_dev // n_lat
    level_shape = (n_lat * rl, nb, padded, block)
    depth = merid_w.shape[0] - 1
    offsets = {}
    levels = 0
    for name in sections:
        offsets[name] = levels
        levels += 1 if name == "slab" else per
    spec = (depth, n_lat, per, x_off, r_off, offsets, a is not None, r is not None)
    fields = [f for f in (a, x, r) if f is not None]
    vmem = pl.BlockSpec(memory_space=pltpu.MemorySpace.VMEM)
    return pl.pallas_call(
        functools.partial(_kernel, spec),
        out_shape=jax.ShapeDtypeStruct((n_dev, levels, rl, block), jnp.float32),
        in_specs=[vmem] * (len(fields) + 2) + [pl.BlockSpec(memory_space=pltpu.MemorySpace.SMEM)],
        out_specs=vmem,
        scratch_shapes=[
            pltpu.VMEM(level_shape, jnp.float32),
            pltpu.VMEM(level_shape, jnp.float32),
            pltpu.VMEM((2 * depth, nb, padded, block), jnp.float32),
        ],
        compiler_params=pltpu.CompilerParams(vmem_limit_bytes=60 * 1024 * 1024),
    )(*fields, table, index, merid_w)


def per_device(gradient, obs_weight, half_width, zonal_coef, mirror_map, merid_coef, vertical_map):
    n_lon = lax.axis_size("lon")
    n_lat = lax.axis_size("lat")
    n_dev = n_lon * n_lat
    lev, rows, cols = gradient.shape
    per = -(-lev // n_dev)
    padded = -(-per // 8) * 8 if per >= 4 else per
    width = zonal_coef.shape[1] - 1
    merid_w = merid_weights(merid_coef)

    def exchange(parts):
        return lax.all_to_all(parts, AXES, 0, 0, tiled=True)

    padded_lev = n_dev * per

    def col_parts(x):
        x = jnp.pad(x, ((0, padded_lev - x.shape[0]), (0, 0), (0, 0)))
        return x.reshape(n_dev, per, rows, cols)

    def to_column(z):
        return z.reshape(padded_lev, rows, cols)

    def to_output(z):
        return z.reshape(padded_lev, rows, cols)[:lev]

    vertical_pad = jnp.pad(vertical_map, ((0, 0), (0, padded_lev - lev)))

    lanes = cols if rows >= 4 else 1

    def slab(values):
        flat = jnp.repeat(values, lanes)
        flat = jnp.zeros((rows * cols,), jnp.float32).at[: flat.shape[0]].set(flat)
        return jnp.broadcast_to(flat.reshape(1, 1, rows, cols), (n_dev, 1, rows, cols))

    def levels_of(sections):
        return sum(1 if name == "slab" else per for name in sections)

    def totals(piece):
        flat = piece.reshape(n_dev, rows * cols)[:, : 4 * lanes].reshape(n_dev, 4, lanes)
        return jnp.sum(flat, axis=0)

    params = jnp.concatenate(
        [mirror_map.astype(jnp.float32), zonal_weights(half_width, zonal_coef).reshape(-1)]
    )
    slab_count = -(-params.shape[0] // (rows * cols))
    params = jnp.pad(params, (0, slab_count * rows * cols - params.shape[0]))
    params = params.reshape(1, slab_count, rows, cols)
    got = exchange(
        jnp.concatenate(
            [col_parts(gradient), jnp.broadcast_to(params, (n_dev, slab_count, rows, cols))], axis=1
        )
    )
    received = got[:, per:].reshape(n_lon, n_lat, slab_count * rows * cols)
    mirror_all = received[:, 0, :cols].reshape(n_lon * cols).astype(jnp.int32)
    zonal_all = received[0, :, cols : cols + rows * (width + 1)].reshape(n_lat * rows, width + 1)
    table = zonal_tables(zonal_all, cols)
    onehot = mirror_tables(mirror_all, cols)

    def apply(sections, a, x, x_off, r=None, r_off=0):
        return level_apply(
            sections, a, x, x_off, r, r_off, table, onehot, merid_w, n_lat, per, padded
        )

    def middle(y):
        lifted = jnp.einsum("kl,lji->kji", vertical_pad, y, precision=KERNEL_PRECISION)
        return jnp.einsum(
            "lk,lji->kji", vertical_pad, obs_weight * lifted, precision=KERNEL_PRECISION
        )

    def lowered(px_col):
        return exchange(col_parts(middle(px_col)))

    res_col = gradient
    inc_col = jnp.zeros_like(gradient)
    res_buf = got
    pres_col = to_column(exchange(apply(("p",), None, res_buf, 0)))
    for outer in range(OUTER):
        last = outer == OUTER - 1
        first_buf = apply(("p", "f"), lowered(pres_col), res_buf, 0)
        got = exchange(first_buf)
        pfirst_col = to_column(got[:, :per])
        first_col = to_output(got[:, per:])
        sections = ("f", "slab") if last else ("f", "p", "slab")
        second_buf = apply(sections, lowered(pfirst_col), first_buf, per, res_buf, 0)
        got = exchange(second_buf)
        second_col = to_output(got[:, :per])
        total = totals(got[:, levels_of(sections) - 1])
        sum_rr, sum_rf, sum_ff, sum_fs = total[0], total[1], total[2], total[3]
        determinant = sum_rf * sum_fs - sum_ff * sum_ff
        coef_one = (sum_fs * sum_rr - sum_ff * sum_rf) / determinant
        coef_two = (sum_rf * sum_rf - sum_ff * sum_rr) / determinant
        inc_col = inc_col + coef_one * res_col + coef_two * first_col
        res_col = res_col - coef_one * first_col - coef_two * second_col
        if not last:
            psecond_col = to_column(got[:, per : 2 * per])
            res_buf = (
                res_buf[:, :per]
                - coef_one * first_buf[:, per : 2 * per]
                - coef_two * second_buf[:, :per]
            )
            pres_col = pres_col - coef_one * pfirst_col - coef_two * psecond_col
    return (inc_col, res_col)


def solution(mesh):
    placed = (
        P(None, "lat", "lon"),
        P(None, "lat", "lon"),
        P("lat"),
        P("lat", None),
        P("lon"),
        P(),
        P(),
    )
    return jax.shard_map(
        per_device,
        mesh=mesh,
        in_specs=placed,
        out_specs=(P(None, "lat", "lon"), P(None, "lat", "lon")),
        check_vma=False,
    )
```

```python
import functools

import jax
import jax.numpy as jnp
from jax import lax
from jax.experimental import pallas as pl
from jax.experimental.pallas import tpu as pltpu
from jax.sharding import PartitionSpec as P

OUTER = 2
AXES = ("lon", "lat")
HI = lax.Precision.HIGHEST
KERNEL_PRECISION = lax.Precision.HIGH


def zonal_weights(half_width, zonal_coef):
    tap_ids = jnp.arange(zonal_coef.shape[1], dtype=jnp.int32)
    kept = jnp.where(
        tap_ids[None, :] <= half_width[:, None], zonal_coef, jnp.zeros_like(zonal_coef)
    )
    scaling = jnp.sqrt(kept[:, 0] ** 2 + 2.0 * jnp.sum(kept[:, 1:] ** 2, axis=1))
    return kept / scaling[:, None]


def merid_weights(merid_coef):
    norm_value = jnp.sqrt(merid_coef[0] ** 2 + 2.0 * jnp.sum(merid_coef[1:] ** 2))
    return merid_coef / norm_value


def zonal_tables(weights, block):
    width = weights.shape[1] - 1
    source = jnp.arange(2 * block, dtype=jnp.int32)
    lane = source % block
    shift = jnp.where(source < block, 0, jnp.where(lane < block // 2, block, -block))
    columns = jnp.arange(block, dtype=jnp.int32)
    tap_ids = jnp.arange(width + 1, dtype=jnp.int32)
    distance = jnp.abs((lane + shift)[:, None] - columns[None, :])
    selector = (distance[:, :, None] == tap_ids[None, None, :]).astype(jnp.float32)
    return jnp.einsum("pct,jt->jpc", selector, weights, precision=KERNEL_PRECISION)


def mirror_tables(mirror_all, block):
    return (mirror_all % block).reshape(mirror_all.shape[0] // block, block)


def _dot(a, b):
    return jnp.dot(a, b, preferred_element_type=jnp.float32, precision=KERNEL_PRECISION)


def _zonal_rows(src, dst, table_ref, add=None):
    rows, nb, lp, block = src.shape
    lane = lax.broadcasted_iota(jnp.int32, (nb * lp, block), 1)
    for j in range(rows):
        mid = src[j]
        prev = jnp.concatenate([mid[nb - 1 :], mid[: nb - 1]], axis=0) if nb > 1 else mid
        nxt = jnp.concatenate([mid[1:], mid[:1]], axis=0) if nb > 1 else mid
        outer = jnp.where(
            lane >= block // 2, prev.reshape(nb * lp, block), nxt.reshape(nb * lp, block)
        )
        acc = _dot(jnp.concatenate([mid.reshape(nb * lp, block), outer], axis=1), table_ref[j])
        acc = acc.reshape(nb, lp, block)
        if add is not None:
            acc = acc + add[j]
        dst[j] = acc


def _merid_rows(src, dst, mir, index_ref, w_ref, depth):
    rows, nb, lp, block = src.shape
    half = nb // 2

    def mirror_block(b, carry):
        sb = lax.rem(b + half, nb)
        polar = jnp.concatenate(
            [src[pl.ds(0, depth), pl.ds(sb, 1)], src[pl.ds(rows - depth, depth), pl.ds(sb, 1)]],
            axis=0,
        )
        source = lax.broadcasted_iota(jnp.int32, (block, block), 0)
        onehot = (source == index_ref[pl.ds(b, 1), :]).astype(jnp.bfloat16)
        polar = polar.reshape(2 * depth * lp, block)
        high = polar.astype(jnp.bfloat16)
        low = (polar - high.astype(jnp.float32)).astype(jnp.bfloat16)
        out = jnp.dot(high, onehot, preferred_element_type=jnp.float32) + jnp.dot(
            low, onehot, preferred_element_type=jnp.float32
        )
        mir[:, pl.ds(b, 1)] = out.reshape(2 * depth, 1, lp, block)
        return carry

    lax.fori_loop(0, nb, mirror_block, 0, unroll=nb <= 16)

    def row(k):
        if k < 0:
            return mir[-1 - k]
        if k >= rows:
            return mir[depth + (rows - 1 - (k - rows)) - (rows - depth)]
        return src[k]

    for j in range(rows):
        acc = w_ref[0] * src[j]
        for o in range(1, depth + 1):
            acc = acc + w_ref[o] * (row(j - o) + row(j + o))
        dst[j] = acc


def _unpack(parts_ref, off, dst, n_lat, per):
    rl = parts_ref.shape[2]
    nb = dst.shape[1]

    def one_block(b, carry):
        for a in range(n_lat):
            for lev in range(per):
                tile = parts_ref[b * n_lat + a, off + lev]
                for r in range(rl):
                    dst[a * rl + r, pl.ds(b, 1), pl.ds(lev, 1), :] = tile[r : r + 1].reshape(1, 1, -1)
        return carry

    lax.fori_loop(0, nb, one_block, 0, unroll=nb <= 16)


def _pack(src, parts_ref, off, n_lat, per):
    rl = parts_ref.shape[2]
    nb = src.shape[1]

    def one_block(b, carry):
        for a in range(n_lat):
            for lev in range(per):
                tile = jnp.concatenate(
                    [src[a * rl + r, pl.ds(b, 1), pl.ds(lev, 1), :].reshape(1, -1) for r in range(rl)],
                    axis=0,
                )
                parts_ref[b * n_lat + a, off + lev] = tile
        return carry

    lax.fori_loop(0, nb, one_block, 0, unroll=nb <= 16)


def _kernel(spec, *refs):
    depth, n_lat, per, x_off, r_off, offsets, has_a, has_r = spec
    refs = list(refs)
    a_ref = refs.pop(0) if has_a else None
    x_ref = refs.pop(0)
    r_ref = refs.pop(0) if has_r else None
    table_ref, index_ref, w_ref, out_ref, u, v, mir = refs
    if a_ref is None:
        _unpack(x_ref, x_off, u, n_lat, per)
        _zonal_rows(u, v, table_ref)
        _merid_rows(v, u, mir, index_ref, w_ref, depth)
        _pack(u, out_ref, offsets["p"], n_lat, per)
        return
    _unpack(a_ref, 0, u, n_lat, per)
    _merid_rows(u, v, mir, index_ref, w_ref, depth)
    _unpack(x_ref, x_off, u, n_lat, per)
    _zonal_rows(v, v, table_ref, add=u)
    _pack(v, out_ref, offsets["f"], n_lat, per)
    if "p" in offsets:
        _zonal_rows(v, u, table_ref)
        _merid_rows(u, v, mir, index_ref, w_ref, depth)
        _pack(v, out_ref, offsets["p"], n_lat, per)
    if "slab" in offsets:
        res = r_ref[:, pl.ds(r_off, per)]
        fst = x_ref[:, pl.ds(x_off, per)]
        snd = out_ref[:, pl.ds(offsets["f"], per)]
        sums = [jnp.sum(res * res), jnp.sum(res * fst), jnp.sum(fst * fst), jnp.sum(fst * snd)]
        n_dev, _, rl, block = out_ref.shape
        row = lax.broadcasted_iota(jnp.int32, (rl, block), 0)
        tile = jnp.zeros((rl, block), jnp.float32)
        for i, value in enumerate(sums):
            tile = jnp.where(row == i, value, tile)
        out_ref[:, offsets["slab"]] = jnp.broadcast_to(tile[None], (n_dev, rl, block))


def level_apply(sections, a, x, x_off, r, r_off, table, index, merid_w, n_lat, per, padded):
    n_dev, _, rl, block = x.shape
    nb = n_dev // n_lat
    level_shape = (n_lat * rl, nb, padded, block)
    depth = merid_w.shape[0] - 1
    offsets = {}
    levels = 0
    for name in sections:
        offsets[name] = levels
        levels += 1 if name == "slab" else per
    spec = (depth, n_lat, per, x_off, r_off, offsets, a is not None, r is not None)
    fields = [f for f in (a, x, r) if f is not None]
    vmem = pl.BlockSpec(memory_space=pltpu.MemorySpace.VMEM)
    return pl.pallas_call(
        functools.partial(_kernel, spec),
        out_shape=jax.ShapeDtypeStruct((n_dev, levels, rl, block), jnp.float32),
        in_specs=[vmem] * (len(fields) + 2) + [pl.BlockSpec(memory_space=pltpu.MemorySpace.SMEM)],
        out_specs=vmem,
        scratch_shapes=[
            pltpu.VMEM(level_shape, jnp.float32),
            pltpu.VMEM(level_shape, jnp.float32),
            pltpu.VMEM((2 * depth, nb, padded, block), jnp.float32),
        ],
        compiler_params=pltpu.CompilerParams(vmem_limit_bytes=60 * 1024 * 1024),
    )(*fields, table, index, merid_w)


def per_device(gradient, obs_weight, half_width, zonal_coef, mirror_map, merid_coef, vertical_map):
    n_lon = lax.axis_size("lon")
    n_lat = lax.axis_size("lat")
    n_dev = n_lon * n_lat
    lev, rows, cols = gradient.shape
    per = -(-lev // n_dev)
    padded = -(-per // 8) * 8 if per >= 4 else per
    width = zonal_coef.shape[1] - 1
    merid_w = merid_weights(merid_coef)

    def exchange(parts):
        return lax.all_to_all(parts, AXES, 0, 0, tiled=True)

    padded_lev = n_dev * per

    def col_parts(x):
        x = jnp.pad(x, ((0, padded_lev - x.shape[0]), (0, 0), (0, 0)))
        return x.reshape(n_dev, per, rows, cols)

    def to_column(z):
        return z.reshape(padded_lev, rows, cols)

    def to_output(z):
        return z.reshape(padded_lev, rows, cols)[:lev]

    vertical_pad = jnp.pad(vertical_map, ((0, 0), (0, padded_lev - lev)))

    lanes = cols if rows >= 4 else 1

    def slab(values):
        flat = jnp.repeat(values, lanes)
        flat = jnp.zeros((rows * cols,), jnp.float32).at[: flat.shape[0]].set(flat)
        return jnp.broadcast_to(flat.reshape(1, 1, rows, cols), (n_dev, 1, rows, cols))

    def levels_of(sections):
        return sum(1 if name == "slab" else per for name in sections)

    def totals(piece):
        flat = piece.reshape(n_dev, rows * cols)[:, : 4 * lanes].reshape(n_dev, 4, lanes)
        return jnp.sum(flat, axis=0)

    params = jnp.concatenate(
        [mirror_map.astype(jnp.float32), zonal_weights(half_width, zonal_coef).reshape(-1)]
    )
    slab_count = -(-params.shape[0] // (rows * cols))
    params = jnp.pad(params, (0, slab_count * rows * cols - params.shape[0]))
    params = params.reshape(1, slab_count, rows, cols)
    got = exchange(
        jnp.concatenate(
            [col_parts(gradient), jnp.broadcast_to(params, (n_dev, slab_count, rows, cols))], axis=1
        )
    )
    received = got[:, per:].reshape(n_lon, n_lat, slab_count * rows * cols)
    mirror_all = received[:, 0, :cols].reshape(n_lon * cols).astype(jnp.int32)
    zonal_all = received[0, :, cols : cols + rows * (width + 1)].reshape(n_lat * rows, width + 1)
    table = zonal_tables(zonal_all, cols)
    onehot = mirror_tables(mirror_all, cols)

    def apply(sections, a, x, x_off, r=None, r_off=0):
        return level_apply(
            sections, a, x, x_off, r, r_off, table, onehot, merid_w, n_lat, per, padded
        )

    def middle(y):
        lifted = jnp.einsum("kl,lji->kji", vertical_pad, y, precision=KERNEL_PRECISION)
        return jnp.einsum(
            "lk,lji->kji", vertical_pad, obs_weight * lifted, precision=KERNEL_PRECISION
        )

    def lowered(px_col):
        return exchange(col_parts(middle(px_col)))

    res_col = gradient
    inc_col = jnp.zeros_like(gradient)
    res_buf = got
    pres_col = to_column(exchange(apply(("p",), None, res_buf, 0)))
    for outer in range(OUTER):
        last = outer == OUTER - 1
        first_buf = apply(("p", "f"), lowered(pres_col), res_buf, 0)
        got = exchange(first_buf)
        pfirst_col = to_column(got[:, :per])
        first_col = to_output(got[:, per:])
        sections = ("f", "slab") if last else ("f", "p", "slab")
        second_buf = apply(sections, lowered(pfirst_col), first_buf, per, res_buf, 0)
        got = exchange(second_buf)
        second_col = to_output(got[:, :per])
        total = totals(got[:, levels_of(sections) - 1])
        sum_rr, sum_rf, sum_ff, sum_fs = total[0], total[1], total[2], total[3]
        determinant = sum_rf * sum_fs - sum_ff * sum_ff
        coef_one = (sum_fs * sum_rr - sum_ff * sum_rf) / determinant
        coef_two = (sum_rf * sum_rf - sum_ff * sum_rr) / determinant
        inc_col = inc_col + coef_one * res_col + coef_two * first_col
        res_col = res_col - coef_one * first_col - coef_two * second_col
        if not last:
            psecond_col = to_column(got[:, per : 2 * per])
            res_buf = (
                res_buf[:, :per]
                - coef_one * first_buf[:, per : 2 * per]
                - coef_two * second_buf[:, :per]
            )
            pres_col = pres_col - coef_one * pfirst_col - coef_two * psecond_col
    return (inc_col, res_col)


def solution(mesh):
    placed = (
        P(None, "lat", "lon"),
        P(None, "lat", "lon"),
        P("lat"),
        P("lat", None),
        P("lon"),
        P(),
        P(),
    )
    return jax.shard_map(
        per_device,
        mesh=mesh,
        in_specs=placed,
        out_specs=(P(None, "lat", "lon"), P(None, "lat", "lon")),
        check_vma=False,
    )
```

```python
import functools

import jax
import jax.numpy as jnp
from jax import lax
from jax.experimental import pallas as pl
from jax.experimental.pallas import tpu as pltpu
from jax.sharding import PartitionSpec as P

OUTER = 2
AXES = ("lon", "lat")
HI = lax.Precision.HIGHEST
KERNEL_PRECISION = lax.Precision.HIGH


def zonal_weights(half_width, zonal_coef):
    tap_ids = jnp.arange(zonal_coef.shape[1], dtype=jnp.int32)
    kept = jnp.where(
        tap_ids[None, :] <= half_width[:, None], zonal_coef, jnp.zeros_like(zonal_coef)
    )
    scaling = jnp.sqrt(kept[:, 0] ** 2 + 2.0 * jnp.sum(kept[:, 1:] ** 2, axis=1))
    return kept / scaling[:, None]


def merid_weights(merid_coef):
    norm_value = jnp.sqrt(merid_coef[0] ** 2 + 2.0 * jnp.sum(merid_coef[1:] ** 2))
    return merid_coef / norm_value


def zonal_tables(weights, block):
    width = weights.shape[1] - 1
    source = jnp.arange(2 * block, dtype=jnp.int32)
    lane = source % block
    shift = jnp.where(source < block, 0, jnp.where(lane < block // 2, block, -block))
    columns = jnp.arange(block, dtype=jnp.int32)
    tap_ids = jnp.arange(width + 1, dtype=jnp.int32)
    distance = jnp.abs((lane + shift)[:, None] - columns[None, :])
    selector = (distance[:, :, None] == tap_ids[None, None, :]).astype(jnp.float32)
    return jnp.einsum("pct,jt->jpc", selector, weights, precision=KERNEL_PRECISION)


def mirror_tables(mirror_all, block):
    return (mirror_all % block).reshape(mirror_all.shape[0] // block, block)


def _dot(a, b):
    return jnp.dot(a, b, preferred_element_type=jnp.float32, precision=KERNEL_PRECISION)


def _zonal_rows(src, dst, table_ref, add=None):
    rows, nb, lp, block = src.shape
    lane = lax.broadcasted_iota(jnp.int32, (nb * lp, block), 1)
    for j in range(rows):
        mid = src[j]
        prev = jnp.concatenate([mid[nb - 1 :], mid[: nb - 1]], axis=0) if nb > 1 else mid
        nxt = jnp.concatenate([mid[1:], mid[:1]], axis=0) if nb > 1 else mid
        outer = jnp.where(
            lane >= block // 2, prev.reshape(nb * lp, block), nxt.reshape(nb * lp, block)
        )
        acc = _dot(jnp.concatenate([mid.reshape(nb * lp, block), outer], axis=1), table_ref[j])
        acc = acc.reshape(nb, lp, block)
        if add is not None:
            acc = acc + add[j]
        dst[j] = acc


def _merid_rows(src, dst, mir, index_ref, w_ref, depth):
    rows, nb, lp, block = src.shape
    half = nb // 2

    def mirror_block(b, carry):
        sb = lax.rem(b + half, nb)
        polar = jnp.concatenate(
            [src[pl.ds(0, depth), pl.ds(sb, 1)], src[pl.ds(rows - depth, depth), pl.ds(sb, 1)]],
            axis=0,
        )
        source = lax.broadcasted_iota(jnp.int32, (block, block), 0)
        onehot = (source == index_ref[pl.ds(b, 1), :]).astype(jnp.bfloat16)
        polar = polar.reshape(2 * depth * lp, block)
        high = polar.astype(jnp.bfloat16)
        low = (polar - high.astype(jnp.float32)).astype(jnp.bfloat16)
        out = jnp.dot(
            jnp.concatenate([high, low], axis=1),
            jnp.concatenate([onehot, onehot], axis=0),
            preferred_element_type=jnp.float32,
        )
        mir[:, pl.ds(b, 1)] = out.reshape(2 * depth, 1, lp, block)
        return carry

    lax.fori_loop(0, nb, mirror_block, 0, unroll=nb <= 16)

    def row(k):
        if k < 0:
            return mir[-1 - k]
        if k >= rows:
            return mir[depth + (rows - 1 - (k - rows)) - (rows - depth)]
        return src[k]

    for j in range(rows):
        acc = w_ref[0] * src[j]
        for o in range(1, depth + 1):
            acc = acc + w_ref[o] * (row(j - o) + row(j + o))
        dst[j] = acc


def _unpack(parts_ref, off, dst, n_lat, per):
    rl = parts_ref.shape[2]
    nb = dst.shape[1]

    def one_block(b, carry):
        for a in range(n_lat):
            for lev in range(per):
                tile = parts_ref[b * n_lat + a, off + lev]
                for r in range(rl):
                    dst[a * rl + r, pl.ds(b, 1), pl.ds(lev, 1), :] = tile[r : r + 1].reshape(1, 1, -1)
        return carry

    lax.fori_loop(0, nb, one_block, 0, unroll=nb <= 16)


def _pack(src, parts_ref, off, n_lat, per):
    rl = parts_ref.shape[2]
    nb = src.shape[1]

    def one_block(b, carry):
        for a in range(n_lat):
            for lev in range(per):
                tile = jnp.concatenate(
                    [src[a * rl + r, pl.ds(b, 1), pl.ds(lev, 1), :].reshape(1, -1) for r in range(rl)],
                    axis=0,
                )
                parts_ref[b * n_lat + a, off + lev] = tile
        return carry

    lax.fori_loop(0, nb, one_block, 0, unroll=nb <= 16)


def _kernel(spec, *refs):
    depth, n_lat, per, x_off, r_off, offsets, has_a, has_r = spec
    refs = list(refs)
    a_ref = refs.pop(0) if has_a else None
    x_ref = refs.pop(0)
    r_ref = refs.pop(0) if has_r else None
    table_ref, index_ref, w_ref, out_ref, u, v, mir = refs
    if a_ref is None:
        _unpack(x_ref, x_off, u, n_lat, per)
        _zonal_rows(u, v, table_ref)
        _merid_rows(v, u, mir, index_ref, w_ref, depth)
        _pack(u, out_ref, offsets["p"], n_lat, per)
        return
    _unpack(a_ref, 0, u, n_lat, per)
    _merid_rows(u, v, mir, index_ref, w_ref, depth)
    _unpack(x_ref, x_off, u, n_lat, per)
    _zonal_rows(v, v, table_ref, add=u)
    _pack(v, out_ref, offsets["f"], n_lat, per)
    if "p" in offsets:
        _zonal_rows(v, u, table_ref)
        _merid_rows(u, v, mir, index_ref, w_ref, depth)
        _pack(v, out_ref, offsets["p"], n_lat, per)
    if "slab" in offsets:
        res = r_ref[:, pl.ds(r_off, per)]
        fst = x_ref[:, pl.ds(x_off, per)]
        snd = out_ref[:, pl.ds(offsets["f"], per)]
        sums = [jnp.sum(res * res), jnp.sum(res * fst), jnp.sum(fst * fst), jnp.sum(fst * snd)]
        n_dev, _, rl, block = out_ref.shape
        row = lax.broadcasted_iota(jnp.int32, (rl, block), 0)
        tile = jnp.zeros((rl, block), jnp.float32)
        for i, value in enumerate(sums):
            tile = jnp.where(row == i, value, tile)
        out_ref[:, offsets["slab"]] = jnp.broadcast_to(tile[None], (n_dev, rl, block))


def level_apply(sections, a, x, x_off, r, r_off, table, index, merid_w, n_lat, per, padded):
    n_dev, _, rl, block = x.shape
    nb = n_dev // n_lat
    level_shape = (n_lat * rl, nb, padded, block)
    depth = merid_w.shape[0] - 1
    offsets = {}
    levels = 0
    for name in sections:
        offsets[name] = levels
        levels += 1 if name == "slab" else per
    spec = (depth, n_lat, per, x_off, r_off, offsets, a is not None, r is not None)
    fields = [f for f in (a, x, r) if f is not None]
    vmem = pl.BlockSpec(memory_space=pltpu.MemorySpace.VMEM)
    return pl.pallas_call(
        functools.partial(_kernel, spec),
        out_shape=jax.ShapeDtypeStruct((n_dev, levels, rl, block), jnp.float32),
        in_specs=[vmem] * (len(fields) + 2) + [pl.BlockSpec(memory_space=pltpu.MemorySpace.SMEM)],
        out_specs=vmem,
        scratch_shapes=[
            pltpu.VMEM(level_shape, jnp.float32),
            pltpu.VMEM(level_shape, jnp.float32),
            pltpu.VMEM((2 * depth, nb, padded, block), jnp.float32),
        ],
        compiler_params=pltpu.CompilerParams(vmem_limit_bytes=60 * 1024 * 1024),
    )(*fields, table, index, merid_w)


def per_device(gradient, obs_weight, half_width, zonal_coef, mirror_map, merid_coef, vertical_map):
    n_lon = lax.axis_size("lon")
    n_lat = lax.axis_size("lat")
    n_dev = n_lon * n_lat
    lev, rows, cols = gradient.shape
    per = -(-lev // n_dev)
    padded = -(-per // 8) * 8 if per >= 4 else per
    width = zonal_coef.shape[1] - 1
    merid_w = merid_weights(merid_coef)

    def exchange(parts):
        return lax.all_to_all(parts, AXES, 0, 0, tiled=True)

    padded_lev = n_dev * per

    def col_parts(x):
        x = jnp.pad(x, ((0, padded_lev - x.shape[0]), (0, 0), (0, 0)))
        return x.reshape(n_dev, per, rows, cols)

    def to_column(z):
        return z.reshape(padded_lev, rows, cols)

    def to_output(z):
        return z.reshape(padded_lev, rows, cols)[:lev]

    vertical_pad = jnp.pad(vertical_map, ((0, 0), (0, padded_lev - lev)))

    lanes = cols if rows >= 4 else 1

    def slab(values):
        flat = jnp.repeat(values, lanes)
        flat = jnp.zeros((rows * cols,), jnp.float32).at[: flat.shape[0]].set(flat)
        return jnp.broadcast_to(flat.reshape(1, 1, rows, cols), (n_dev, 1, rows, cols))

    def levels_of(sections):
        return sum(1 if name == "slab" else per for name in sections)

    def totals(piece):
        flat = piece.reshape(n_dev, rows * cols)[:, : 4 * lanes].reshape(n_dev, 4, lanes)
        return jnp.sum(flat, axis=0)

    params = jnp.concatenate(
        [mirror_map.astype(jnp.float32), zonal_weights(half_width, zonal_coef).reshape(-1)]
    )
    slab_count = -(-params.shape[0] // (rows * cols))
    params = jnp.pad(params, (0, slab_count * rows * cols - params.shape[0]))
    params = params.reshape(1, slab_count, rows, cols)
    got = exchange(
        jnp.concatenate(
            [col_parts(gradient), jnp.broadcast_to(params, (n_dev, slab_count, rows, cols))], axis=1
        )
    )
    received = got[:, per:].reshape(n_lon, n_lat, slab_count * rows * cols)
    mirror_all = received[:, 0, :cols].reshape(n_lon * cols).astype(jnp.int32)
    zonal_all = received[0, :, cols : cols + rows * (width + 1)].reshape(n_lat * rows, width + 1)
    table = zonal_tables(zonal_all, cols)
    onehot = mirror_tables(mirror_all, cols)

    def apply(sections, a, x, x_off, r=None, r_off=0):
        return level_apply(
            sections, a, x, x_off, r, r_off, table, onehot, merid_w, n_lat, per, padded
        )

    def middle(y):
        lifted = jnp.einsum("kl,lji->kji", vertical_pad, y, precision=KERNEL_PRECISION)
        return jnp.einsum(
            "lk,lji->kji", vertical_pad, obs_weight * lifted, precision=KERNEL_PRECISION
        )

    def lowered(px_col):
        return exchange(col_parts(middle(px_col)))

    res_col = gradient
    inc_col = jnp.zeros_like(gradient)
    res_buf = got
    pres_col = to_column(exchange(apply(("p",), None, res_buf, 0)))
    for outer in range(OUTER):
        last = outer == OUTER - 1
        first_buf = apply(("p", "f"), lowered(pres_col), res_buf, 0)
        got = exchange(first_buf)
        pfirst_col = to_column(got[:, :per])
        first_col = to_output(got[:, per:])
        sections = ("f", "slab") if last else ("f", "p", "slab")
        second_buf = apply(sections, lowered(pfirst_col), first_buf, per, res_buf, 0)
        got = exchange(second_buf)
        second_col = to_output(got[:, :per])
        total = totals(got[:, levels_of(sections) - 1])
        sum_rr, sum_rf, sum_ff, sum_fs = total[0], total[1], total[2], total[3]
        determinant = sum_rf * sum_fs - sum_ff * sum_ff
        coef_one = (sum_fs * sum_rr - sum_ff * sum_rf) / determinant
        coef_two = (sum_rf * sum_rf - sum_ff * sum_rr) / determinant
        inc_col = inc_col + coef_one * res_col + coef_two * first_col
        res_col = res_col - coef_one * first_col - coef_two * second_col
        if not last:
            psecond_col = to_column(got[:, per : 2 * per])
            res_buf = (
                res_buf[:, :per]
                - coef_one * first_buf[:, per : 2 * per]
                - coef_two * second_buf[:, :per]
            )
            pres_col = pres_col - coef_one * pfirst_col - coef_two * psecond_col
    return (inc_col, res_col)


def solution(mesh):
    placed = (
        P(None, "lat", "lon"),
        P(None, "lat", "lon"),
        P("lat"),
        P("lat", None),
        P("lon"),
        P(),
        P(),
    )
    return jax.shard_map(
        per_device,
        mesh=mesh,
        in_specs=placed,
        out_specs=(P(None, "lat", "lon"), P(None, "lat", "lon")),
        check_vma=False,
    )
```
